512 devices in a mesh: dom: 128 (over x, z, core), feat: 4 (over y).
Axes of the slice: x: 4, y: 4, z: 16, core: 2. Of those that a mesh axis runs over, the one named last changes fastest.
Arguments:
- replica_feat: bfloat16 [256, 262144], P('feat', 'dom'), may hold values from -6 to 6
- adjacency_tiles: bfloat16 [12288, 128, 128], P('dom'), may hold values from 0.0019989014 to 0.049804688
- tile_index: int32 [2, 12288], P(None, 'dom'), may hold values from -1 to 15, as said below
- route: int32 [1, 262144], P(None, 'dom'), may hold values from -1 to 2047, as said below
- node_feat: bfloat16 [256, 262144], P('feat', 'dom'), may hold values from -6 to 6
- w_self: bfloat16 [256, 256], replicated, may hold values from -0.375 to 0.375
- w_neigh: bfloat16 [256, 256], replicated, may hold values from -0.375 to 0.375
Outputs:
- renewed: bfloat16 [256, 262144], P('feat', 'dom')
- replicas: bfloat16 [256, 262144], P('feat', 'dom')
The draws below stay inside these ranges and needn't reach their ends.
Inputs may be any that keep to these rules, and one draw needn't show every extreme that they name: `tile_index`: row 0 names the destination block and row 1 the source block, among the 16 blocks of 128 slots of its device, of each of a device's 96 tiles; a destination of -1 marks a padding tile, padding tiles come last, at least half of a device's tiles are live and some device has all of them live. `route`: for slot c of group p (groups of 16) of a device's slots: the row, among owner p's 2048 master nodes, of the node that the slot copies, or -1 for an empty slot; rows within a group are distinct, live slots come first, every group has one or more live slots, and some owner has all 16 slots live on every device.
All inputs are finite; a program needn't handle non-finite values.
Results may differ from the reference program's by a relative error of at most 0.0043.
Values may be sent and summed in bfloat16 or wider, within the bound.
A program may use at most 64 MiB of HBM per device.

```python
import math
import jax
import jax.numpy as jnp
from jax import lax

F = 256
TILE = 128
NODE_DEV = 2048
REP_DEV = 2048
TILE_DEV = 96
CAP = 16
NB = 16
NODES = 262144
SLOTS = 262144
TILES = 12288
N_DOM = 128


def draw_route(key, part):
    key_counts, key_full, key_rows = jax.random.split(key, 3)
    counts = jax.random.randint(key_counts, (N_DOM, N_DOM), 1, CAP + 1)
    full = jax.random.randint(key_full, (), 0, N_DOM)
    owner = jnp.arange(N_DOM)[None, :]
    sender = jnp.arange(N_DOM)[:, None]
    counts = jnp.where(owner == full, CAP, counts)
    counts = jnp.where((sender == 0) & (owner == (full + 1) % N_DOM), 1, counts)
    keyset = jax.random.split(key_rows, N_DOM * N_DOM)
    rows = jax.vmap(lambda keyed: jax.random.permutation(keyed, NODE_DEV)[:CAP])(keyset)
    rows = rows.reshape(N_DOM, N_DOM, CAP)
    forced = NODE_DEV - 1 - jnp.arange(CAP)
    rows = jnp.where(((sender == 0) & (owner == full))[:, :, None], forced[None, None, :], rows)
    position = jnp.arange(CAP)[None, None, :]
    result = jnp.where(position < counts[:, :, None], rows, -1)
    return result.reshape(1, N_DOM * N_DOM * CAP).astype(jnp.int32)


def draw_tile_index(key, part):
    key_live, key_top, key_dst, key_src = jax.random.split(key, 4)
    live = jax.random.randint(key_live, (N_DOM,), TILE_DEV // 2, TILE_DEV + 1)
    top = jax.random.randint(key_top, (), 0, N_DOM)
    live = jnp.where(jnp.arange(N_DOM) == top, TILE_DEV, live)
    target = jax.random.randint(key_dst, (N_DOM, TILE_DEV), 0, NB)
    source = jax.random.randint(key_src, (N_DOM, TILE_DEV), 0, NB)
    target = target.at[0, 0].set(NB - 1)
    source = source.at[0, 1].set(NB - 1)
    position = jnp.arange(TILE_DEV)[None, :]
    target = jnp.where(position < live[:, None], target, -1)
    return jnp.stack([target, source]).reshape(2, N_DOM * TILE_DEV).astype(jnp.int32)


def block_scale(stream_key, dims, cuts, smallest, largest):
    def one(axis_at, blocks):
        heights = jax.random.uniform(jax.random.fold_in(jax.random.fold_in(stream_key, 6), axis_at), (blocks,), jnp.float32, smallest / len(cuts), largest / len(cuts))
        return jnp.repeat(jnp.exp(heights), dims[axis_at] // blocks).reshape((-1,) + (1,) * (len(dims) - axis_at - 1))

    level = one(*cuts[0])
    for cut in cuts[1:]:
        level = level * one(*cut)
    return level


def centred(stream_key, shape, spread, most, shards=(), kind=jnp.bfloat16):
    level = block_scale(stream_key, shape, shards, -0.22, 0.18) if shards else 1.0
    array = jax.random.normal(stream_key, shape, jnp.float32) * spread * level
    return jnp.minimum(jnp.maximum(array, -most), most).astype(kind)


def setup_inputs(seed: int = 0) -> dict:
    arg_keys = jax.random.split(jax.random.key(seed), 8)
    replica_feat = centred(arg_keys[0], (F, SLOTS), 1.0, 6.0, ((0, 4), (1, 128)))
    adjacency_tiles = jnp.clip(jnp.exp(math.log(0.049804688) - 3.2155114 * jax.random.uniform(arg_keys[1], (TILES, TILE, TILE), jnp.float32) ** block_scale(arg_keys[1], (TILES, TILE, TILE), ((0, 128),), -0.2, 0.2)), 0.0019989014, 0.049804688).astype(jnp.bfloat16)
    tile_index = draw_tile_index(jax.random.fold_in(arg_keys[7], 71), 0)
    route = draw_route(jax.random.fold_in(arg_keys[7], 71), 0)
    node_feat = centred(arg_keys[4], (F, NODES), 1.0, 6.0, ((0, 4), (1, 128)))
    w_self = centred(arg_keys[5], (F, F), F ** -0.5, 0.375)
    w_neigh = centred(arg_keys[6], (F, F), F ** -0.5, 0.375)
    return {"replica_feat": replica_feat, "adjacency_tiles": adjacency_tiles, "tile_index": tile_index, "route": route, "node_feat": node_feat, "w_self": w_self, "w_neigh": w_neigh}


def reference(replica_feat, adjacency_tiles, tile_index, route, node_feat, w_self, w_neigh):
    block_count = REP_DEV // TILE

    def per_device(device):
        feat_dev = lax.dynamic_slice_in_dim(replica_feat, device * REP_DEV, REP_DEV, 1).astype(jnp.float32)
        feat_dev = feat_dev.reshape(F, block_count, TILE)
        tile_dev = lax.dynamic_slice_in_dim(adjacency_tiles, device * TILE_DEV, TILE_DEV, 0).astype(jnp.float32)
        index_dev = lax.dynamic_slice_in_dim(tile_index, device * TILE_DEV, TILE_DEV, 1)
        picked = jnp.take(feat_dev, index_dev[1], axis=1)
        product = jnp.einsum('ftj,tij->fti', picked, tile_dev)
        one_hot = (index_dev[0][:, None] == jnp.arange(block_count, dtype=jnp.int32)[None, :]).astype(jnp.float32)
        summed = jnp.einsum('fti,tb->fbi', product, one_hot, precision=lax.Precision.HIGHEST)
        return summed.reshape(F, REP_DEV).astype(jnp.bfloat16)

    partials = lax.map(per_device, jnp.arange(N_DOM, dtype=jnp.int32))
    flat = partials.transpose(0, 2, 1).reshape(SLOTS, F).astype(jnp.float32)
    owner = ((jnp.arange(SLOTS, dtype=jnp.int32) // CAP) % N_DOM).astype(jnp.int32)
    live = route[0] >= 0
    target = jnp.where(live, owner * NODE_DEV + route[0], NODES).astype(jnp.int32)
    agg = jax.ops.segment_sum(flat, target, num_segments=NODES + 1)[:NODES].T.astype(jnp.bfloat16)
    preact = jnp.dot(w_self.T, node_feat, preferred_element_type=jnp.float32)
    preact = preact + jnp.dot(w_neigh.T, agg, preferred_element_type=jnp.float32)
    renewed = jnp.maximum(preact, jnp.float32(0.0)).astype(jnp.bfloat16)
    chosen = jnp.take(renewed, jnp.minimum(target, NODES - 1).astype(jnp.int32), axis=1)
    replicas = jnp.where(live[None, :], chosen, jnp.zeros_like(chosen)).astype(jnp.bfloat16)
    return (renewed, replicas)
```

```python
import functools

import jax
import jax.numpy as jnp
from jax import lax
from jax.experimental import pallas as pl
from jax.experimental.pallas import tpu as pltpu
from jax.sharding import PartitionSpec as P

MESH = pl.DeviceIdType.MESH


def _a2a_kernel(x_ref, o_ref, send_sem, recv_sem, local_sem):
    n = x_ref.shape[0]
    me = lax.axis_index("dom")
    f = lax.axis_index("feat")
    local = pltpu.make_async_copy(x_ref.at[me], o_ref.at[me], local_sem)
    local.start()

    def start(k, carry):
        peer = lax.rem(me + k, n)
        pltpu.make_async_remote_copy(
            x_ref.at[peer],
            o_ref.at[me],
            send_sem.at[peer],
            recv_sem.at[me],
            device_id=(peer, f),
            device_id_type=MESH,
        ).start()
        return carry

    lax.fori_loop(1, n, start, 0)

    def wait(k, carry):
        peer = lax.rem(me + k, n)
        src = lax.rem(me + n - k, n)
        pltpu.make_async_remote_copy(
            x_ref.at[peer],
            o_ref.at[me],
            send_sem.at[peer],
            recv_sem.at[me],
            device_id=(peer, f),
            device_id_type=MESH,
        ).wait_send()
        pltpu.make_async_remote_copy(
            x_ref.at[src],
            o_ref.at[src],
            send_sem.at[src],
            recv_sem.at[src],
            device_id=(src, f),
            device_id_type=MESH,
        ).wait_recv()
        return carry

    lax.fori_loop(1, n, wait, 0)
    local.wait()


def _all_to_all(chunks):
    n = chunks.shape[0]
    return pl.pallas_call(
        _a2a_kernel,
        out_shape=jax.ShapeDtypeStruct(chunks.shape, chunks.dtype),
        in_specs=[pl.BlockSpec(memory_space=pl.ANY)],
        out_specs=pl.BlockSpec(memory_space=pl.ANY),
        scratch_shapes=[
            pltpu.SemaphoreType.DMA((n,)),
            pltpu.SemaphoreType.DMA((n,)),
            pltpu.SemaphoreType.DMA(()),
        ],
        compiler_params=pltpu.CompilerParams(has_side_effects=True),
    )(chunks)


def _exchange(rows, n):
    width, slots = rows.shape
    group = slots // n
    chunks = rows.reshape(width, n, group).transpose(1, 0, 2).reshape(n, width * group // 128, 128)
    got = _all_to_all(chunks)
    return got.reshape(n, width, group).transpose(1, 0, 2).reshape(width, slots)


def per_device(n_dom, replica_feat, adjacency_tiles, tile_index, route, node_feat, w_self, w_neigh):
    feat_width, slot_count = replica_feat.shape
    tile_side = adjacency_tiles.shape[1]
    block_count = slot_count // tile_side
    node_count = node_feat.shape[1]
    full_feat = lax.all_gather(node_feat, "feat", axis=0, tiled=True)
    arrived = lax.all_to_all(route, "dom", split_axis=1, concat_axis=1, tiled=True)
    stacked = replica_feat.reshape(feat_width, block_count, tile_side)
    picked = jnp.take(stacked, tile_index[1], axis=1)
    product = jnp.einsum(
        "ftj,tij->fti", picked, adjacency_tiles, preferred_element_type=jnp.float32
    )
    one_hot = (tile_index[0][:, None] == jnp.arange(block_count, dtype=jnp.int32)[None, :]).astype(
        jnp.float32
    )
    partial_rows = jnp.einsum("fti,tb->fbi", product, one_hot, precision=lax.Precision.HIGHEST)
    partial_rows = partial_rows.reshape(feat_width, slot_count).astype(jnp.bfloat16)
    received = _exchange(partial_rows, n_dom)
    chooser = (arrived[0][:, None] == jnp.arange(node_count, dtype=jnp.int32)[None, :]).astype(
        jnp.bfloat16
    )
    agg = jnp.dot(received, chooser, preferred_element_type=jnp.float32).astype(jnp.bfloat16)
    contract = (((0,), (0,)), ((), ()))
    offset = lax.axis_index("feat") * feat_width
    full_agg = lax.all_gather(agg, "feat", axis=0, tiled=True)
    self_cols = lax.dynamic_slice_in_dim(w_self, offset, feat_width, 1)
    neigh_cols = lax.dynamic_slice_in_dim(w_neigh, offset, feat_width, 1)
    preact = lax.dot_general(self_cols, full_feat, contract, preferred_element_type=jnp.float32)
    preact = preact + lax.dot_general(
        neigh_cols, full_agg, contract, preferred_element_type=jnp.float32
    )
    renewed = jnp.maximum(preact, jnp.float32(0.0)).astype(jnp.bfloat16)
    gathered_rows = lax.dot_general(
        renewed, chooser, (((1,), (1,)), ((), ())), preferred_element_type=jnp.float32
    ).astype(jnp.bfloat16)
    replicas = _exchange(gathered_rows, n_dom)
    return (renewed, replicas)


def solution(mesh):
    in_specs = (
        P("feat", "dom"),
        P("dom", None, None),
        P(None, "dom"),
        P(None, "dom"),
        P("feat", "dom"),
        P(),
        P(),
    )
    out_specs = (P("feat", "dom"), P("feat", "dom"))
    return jax.shard_map(
        functools.partial(per_device, mesh.shape["dom"]), mesh=mesh, in_specs=in_specs, out_specs=out_specs, check_vma=False
    )
```

```python
import functools

import jax
import jax.numpy as jnp
from jax import lax
from jax.experimental import pallas as pl
from jax.experimental.pallas import tpu as pltpu
from jax.sharding import PartitionSpec as P

MESH = pl.DeviceIdType.MESH


def _greet(axis, n, where):
    me = lax.axis_index(axis)
    bar = pltpu.get_barrier_semaphore()

    def sig(k, carry):
        pl.semaphore_signal(bar, 1, device_id=where(lax.rem(me + k, n)), device_id_type=MESH)
        return carry

    lax.fori_loop(1, n, sig, 0)
    pl.semaphore_wait(bar, n - 1)
    return me


def _a2a_kernel(*refs):
    k = (len(refs) - 3) // 2
    xs, outs = refs[:k], refs[k : 2 * k]
    send_sem, recv_sem, local_sem = refs[2 * k :]
    n = xs[0].shape[0]
    f = lax.axis_index("feat")
    where = lambda d: (d, f)
    me = _greet("dom", n, where)
    locals_ = []
    for i in range(k):
        c = pltpu.make_async_copy(xs[i].at[me], outs[i].at[me], local_sem.at[i])
        c.start()
        locals_.append(c)

    def copy(i, peer, src_slot, dst_slot, s_idx, r_idx):
        return pltpu.make_async_remote_copy(
            xs[i].at[src_slot],
            outs[i].at[dst_slot],
            send_sem.at[i, s_idx],
            recv_sem.at[i, r_idx],
            device_id=where(peer),
            device_id_type=MESH,
        )

    def start(j, carry):
        peer = lax.rem(me + j, n)
        for i in range(k):
            copy(i, peer, peer, me, peer, me).start()
        return carry

    lax.fori_loop(1, n, start, 0)

    def wait(j, carry):
        peer = lax.rem(me + j, n)
        src = lax.rem(me + n - j, n)
        for i in range(k):
            copy(i, peer, peer, me, peer, me).wait_send()
            copy(i, src, src, src, src, src).wait_recv()
        return carry

    lax.fori_loop(1, n, wait, 0)
    for c in locals_:
        c.wait()


def _all_to_all(arrays, cid):
    n = arrays[0].shape[0]
    k = len(arrays)
    return pl.pallas_call(
        _a2a_kernel,
        out_shape=[jax.ShapeDtypeStruct(a.shape, a.dtype) for a in arrays],
        in_specs=[pl.BlockSpec(memory_space=pl.ANY)] * k,
        out_specs=[pl.BlockSpec(memory_space=pl.ANY)] * k,
        scratch_shapes=[
            pltpu.SemaphoreType.DMA((k, n)),
            pltpu.SemaphoreType.DMA((k, n)),
            pltpu.SemaphoreType.DMA((k,)),
        ],
        compiler_params=pltpu.CompilerParams(has_side_effects=True, collective_id=cid),
    )(*arrays)


def _gather_kernel(x_ref, o_ref, send_sem, recv_sem, local_sem):
    g = o_ref.shape[0]
    d = lax.axis_index("dom")
    where = lambda q: (d, q)
    me = _greet("feat", g, where)
    local = pltpu.make_async_copy(x_ref, o_ref.at[me], local_sem)
    local.start()

    def copy(peer, slot, s_idx):
        return pltpu.make_async_remote_copy(
            x_ref,
            o_ref.at[slot],
            send_sem.at[s_idx],
            recv_sem.at[slot],
            device_id=where(peer),
            device_id_type=MESH,
        )

    def start(j, carry):
        peer = lax.rem(me + j, g)
        copy(peer, me, peer).start()
        return carry

    lax.fori_loop(1, g, start, 0)

    def wait(j, carry):
        peer = lax.rem(me + j, g)
        src = lax.rem(me + g - j, g)
        copy(peer, me, peer).wait_send()
        copy(src, src, src).wait_recv()
        return carry

    lax.fori_loop(1, g, wait, 0)
    local.wait()


def _feat_gather(x, g, cid):
    return pl.pallas_call(
        _gather_kernel,
        out_shape=jax.ShapeDtypeStruct((g,) + x.shape, x.dtype),
        in_specs=[pl.BlockSpec(memory_space=pl.ANY)],
        out_specs=pl.BlockSpec(memory_space=pl.ANY),
        scratch_shapes=[
            pltpu.SemaphoreType.DMA((g,)),
            pltpu.SemaphoreType.DMA((g,)),
            pltpu.SemaphoreType.DMA(()),
        ],
        compiler_params=pltpu.CompilerParams(has_side_effects=True, collective_id=cid),
    )(x).reshape((g * x.shape[0],) + x.shape[1:])


def _to_chunks(rows, n):
    width, slots = rows.shape
    group = slots // n
    return rows.reshape(width, n, group).transpose(1, 0, 2).reshape(n, width * group // 128, 128)


def _from_chunks(chunks, width):
    n = chunks.shape[0]
    return chunks.reshape(n, width, -1).transpose(1, 0, 2).reshape(width, -1)


def per_device(n_dom, n_feat, replica_feat, adjacency_tiles, tile_index, route, node_feat, w_self, w_neigh):
    feat_width, slot_count = replica_feat.shape
    tile_side = adjacency_tiles.shape[1]
    block_count = slot_count // tile_side
    node_count = node_feat.shape[1]
    full_feat = lax.all_gather(node_feat, "feat", axis=0, tiled=True)
    stacked = replica_feat.reshape(feat_width, block_count, tile_side)
    picked = jnp.take(stacked, tile_index[1], axis=1)
    product = jnp.einsum(
        "ftj,tij->fti", picked, adjacency_tiles, preferred_element_type=jnp.float32
    )
    one_hot = (tile_index[0][:, None] == jnp.arange(block_count, dtype=jnp.int32)[None, :]).astype(
        jnp.float32
    )
    partial_rows = jnp.einsum("fti,tb->fbi", product, one_hot, precision=lax.Precision.HIGHEST)
    partial_rows = partial_rows.reshape(feat_width, slot_count).astype(jnp.bfloat16)
    got, got_route = _all_to_all(
        [_to_chunks(partial_rows, n_dom), route.reshape(n_dom, 1, slot_count // n_dom)], 0
    )
    received = _from_chunks(got, feat_width)
    arrived = got_route.reshape(slot_count)
    chooser = (arrived[:, None] == jnp.arange(node_count, dtype=jnp.int32)[None, :]).astype(
        jnp.bfloat16
    )
    agg = jnp.dot(received, chooser, preferred_element_type=jnp.float32).astype(jnp.bfloat16)
    contract = (((0,), (0,)), ((), ()))
    offset = lax.axis_index("feat") * feat_width
    full_agg = _feat_gather(agg, n_feat, 1)
    self_cols = lax.dynamic_slice_in_dim(w_self, offset, feat_width, 1)
    neigh_cols = lax.dynamic_slice_in_dim(w_neigh, offset, feat_width, 1)
    preact = lax.dot_general(self_cols, full_feat, contract, preferred_element_type=jnp.float32)
    preact = preact + lax.dot_general(
        neigh_cols, full_agg, contract, preferred_element_type=jnp.float32
    )
    renewed = jnp.maximum(preact, jnp.float32(0.0)).astype(jnp.bfloat16)
    gathered_rows = lax.dot_general(
        renewed, chooser, (((1,), (1,)), ((), ())), preferred_element_type=jnp.float32
    ).astype(jnp.bfloat16)
    (back,) = _all_to_all([_to_chunks(gathered_rows, n_dom)], 2)
    replicas = _from_chunks(back, feat_width)
    return (renewed, replicas)


def solution(mesh):
    in_specs = (
        P("feat", "dom"),
        P("dom", None, None),
        P(None, "dom"),
        P(None, "dom"),
        P("feat", "dom"),
        P(),
        P(),
    )
    out_specs = (P("feat", "dom"), P("feat", "dom"))
    body = functools.partial(per_device, mesh.shape["dom"], mesh.shape["feat"])
    return jax.shard_map(body, mesh=mesh, in_specs=in_specs, out_specs=out_specs, check_vma=False)
```

```python
import functools

import jax
import jax.numpy as jnp
from jax import lax
from jax.experimental import pallas as pl
from jax.experimental.pallas import tpu as pltpu
from jax.sharding import PartitionSpec as P

MESH = pl.DeviceIdType.MESH


def _greet(axis, n, where):
    me = lax.axis_index(axis)
    bar = pltpu.get_barrier_semaphore()

    def sig(k, carry):
        pl.semaphore_signal(bar, 1, device_id=where(lax.rem(me + k, n)), device_id_type=MESH)
        return carry

    lax.fori_loop(1, n, sig, 0)
    pl.semaphore_wait(bar, n - 1)
    return me


def _step(j, n):
    half = (j + 1) // 2
    odd = j % 2
    return half * odd + (n - half) * (1 - odd)


def _a2a_kernel(*refs):
    k = (len(refs) - 3) // 2
    xs, outs = refs[:k], refs[k : 2 * k]
    send_sem, recv_sem, local_sem = refs[2 * k :]
    n = xs[0].shape[0]
    f = lax.axis_index("feat")
    where = lambda d: (d, f)
    me = _greet("dom", n, where)
    locals_ = []
    for i in range(k):
        c = pltpu.make_async_copy(xs[i].at[me], outs[i].at[me], local_sem.at[i])
        c.start()
        locals_.append(c)

    def copy(i, peer, src_slot, dst_slot, s_idx, r_idx):
        return pltpu.make_async_remote_copy(
            xs[i].at[src_slot],
            outs[i].at[dst_slot],
            send_sem.at[i, s_idx],
            recv_sem.at[i, r_idx],
            device_id=where(peer),
            device_id_type=MESH,
        )

    def start(j, carry):
        peer = lax.rem(me + _step(j, n), n)
        for i in range(k):
            copy(i, peer, peer, me, peer, me).start()
        return carry

    lax.fori_loop(1, n, start, 0)

    def wait(j, carry):
        peer = lax.rem(me + _step(j, n), n)
        src = lax.rem(me + n - _step(j, n), n)
        for i in range(k):
            copy(i, peer, peer, me, peer, me).wait_send()
            copy(i, src, src, src, src, src).wait_recv()
        return carry

    lax.fori_loop(1, n, wait, 0)
    for c in locals_:
        c.wait()


def _all_to_all(arrays, cid):
    n = arrays[0].shape[0]
    k = len(arrays)
    return pl.pallas_call(
        _a2a_kernel,
        out_shape=[jax.ShapeDtypeStruct(a.shape, a.dtype) for a in arrays],
        in_specs=[pl.BlockSpec(memory_space=pl.ANY)] * k,
        out_specs=[pl.BlockSpec(memory_space=pl.ANY)] * k,
        scratch_shapes=[
            pltpu.SemaphoreType.DMA((k, n)),
            pltpu.SemaphoreType.DMA((k, n)),
            pltpu.SemaphoreType.DMA((k,)),
        ],
        compiler_params=pltpu.CompilerParams(has_side_effects=True, collective_id=cid),
    )(*arrays)


def _gather_kernel(x_ref, o_ref, send_sem, recv_sem, local_sem):
    g = o_ref.shape[0]
    d = lax.axis_index("dom")
    where = lambda q: (d, q)
    me = _greet("feat", g, where)
    local = pltpu.make_async_copy(x_ref, o_ref.at[me], local_sem)
    local.start()

    def copy(peer, slot, s_idx):
        return pltpu.make_async_remote_copy(
            x_ref,
            o_ref.at[slot],
            send_sem.at[s_idx],
            recv_sem.at[slot],
            device_id=where(peer),
            device_id_type=MESH,
        )

    def start(j, carry):
        peer = lax.rem(me + j, g)
        copy(peer, me, peer).start()
        return carry

    lax.fori_loop(1, g, start, 0)

    def wait(j, carry):
        peer = lax.rem(me + j, g)
        src = lax.rem(me + g - j, g)
        copy(peer, me, peer).wait_send()
        copy(src, src, src).wait_recv()
        return carry

    lax.fori_loop(1, g, wait, 0)
    local.wait()


def _feat_gather(x, g, cid):
    return pl.pallas_call(
        _gather_kernel,
        out_shape=jax.ShapeDtypeStruct((g,) + x.shape, x.dtype),
        in_specs=[pl.BlockSpec(memory_space=pl.ANY)],
        out_specs=pl.BlockSpec(memory_space=pl.ANY),
        scratch_shapes=[
            pltpu.SemaphoreType.DMA((g,)),
            pltpu.SemaphoreType.DMA((g,)),
            pltpu.SemaphoreType.DMA(()),
        ],
        compiler_params=pltpu.CompilerParams(has_side_effects=True, collective_id=cid),
    )(x).reshape((g * x.shape[0],) + x.shape[1:])


def _to_chunks(rows, n):
    width, slots = rows.shape
    group = slots // n
    return rows.reshape(width, n, group).transpose(1, 0, 2).reshape(n, width * group // 128, 128)


def _from_chunks(chunks, width):
    n = chunks.shape[0]
    return chunks.reshape(n, width, -1).transpose(1, 0, 2).reshape(width, -1)


def per_device(n_dom, n_feat, replica_feat, adjacency_tiles, tile_index, route, node_feat, w_self, w_neigh):
    feat_width, slot_count = replica_feat.shape
    tile_side = adjacency_tiles.shape[1]
    block_count = slot_count // tile_side
    node_count = node_feat.shape[1]
    full_feat = lax.all_gather(node_feat, "feat", axis=0, tiled=True)
    stacked = replica_feat.reshape(feat_width, block_count, tile_side)
    picked = jnp.take(stacked, tile_index[1], axis=1)
    product = jnp.einsum(
        "ftj,tij->fti", picked, adjacency_tiles, preferred_element_type=jnp.float32
    )
    one_hot = (tile_index[0][:, None] == jnp.arange(block_count, dtype=jnp.int32)[None, :]).astype(
        jnp.float32
    )
    partial_rows = jnp.einsum("fti,tb->fbi", product, one_hot, precision=lax.Precision.HIGHEST)
    partial_rows = partial_rows.reshape(feat_width, slot_count).astype(jnp.bfloat16)
    got, got_route = _all_to_all(
        [_to_chunks(partial_rows, n_dom), route.reshape(n_dom, 1, slot_count // n_dom)], 0
    )
    received = _from_chunks(got, feat_width)
    arrived = got_route.reshape(slot_count)
    chooser = (arrived[:, None] == jnp.arange(node_count, dtype=jnp.int32)[None, :]).astype(
        jnp.bfloat16
    )
    agg = jnp.dot(received, chooser, preferred_element_type=jnp.float32).astype(jnp.bfloat16)
    contract = (((0,), (0,)), ((), ()))
    offset = lax.axis_index("feat") * feat_width
    full_agg = _feat_gather(agg, n_feat, 1)
    self_cols = lax.dynamic_slice_in_dim(w_self, offset, feat_width, 1)
    neigh_cols = lax.dynamic_slice_in_dim(w_neigh, offset, feat_width, 1)
    preact = lax.dot_general(self_cols, full_feat, contract, preferred_element_type=jnp.float32)
    preact = preact + lax.dot_general(
        neigh_cols, full_agg, contract, preferred_element_type=jnp.float32
    )
    renewed = jnp.maximum(preact, jnp.float32(0.0)).astype(jnp.bfloat16)
    gathered_rows = lax.dot_general(
        renewed, chooser, (((1,), (1,)), ((), ())), preferred_element_type=jnp.float32
    ).astype(jnp.bfloat16)
    (back,) = _all_to_all([_to_chunks(gathered_rows, n_dom)], 2)
    replicas = _from_chunks(back, feat_width)
    return (renewed, replicas)


def solution(mesh):
    in_specs = (
        P("feat", "dom"),
        P("dom", None, None),
        P(None, "dom"),
        P(None, "dom"),
        P("feat", "dom"),
        P(),
        P(),
    )
    out_specs = (P("feat", "dom"), P("feat", "dom"))
    body = functools.partial(per_device, mesh.shape["dom"], mesh.shape["feat"])
    return jax.shard_map(body, mesh=mesh, in_specs=in_specs, out_specs=out_specs, check_vma=False)
```

```python
import functools

import jax
import jax.numpy as jnp
from jax import lax
from jax.experimental import pallas as pl
from jax.experimental.pallas import tpu as pltpu
from jax.sharding import PartitionSpec as P

MESH = pl.DeviceIdType.MESH


def _greet(axis, n, where):
    me = lax.axis_index(axis)
    bar = pltpu.get_barrier_semaphore()

    def sig(k, carry):
        pl.semaphore_signal(bar, 1, device_id=where(lax.rem(me + k, n)), device_id_type=MESH)
        return carry

    lax.fori_loop(1, n, sig, 0)
    pl.semaphore_wait(bar, n - 1)
    return me


def _step(j, n):
    half = (j + 1) // 2
    odd = j % 2
    return half * odd + (n - half) * (1 - odd)


def _a2a_kernel(*refs):
    k = (len(refs) - 2) // 2
    xs, outs = refs[:k], refs[k : 2 * k]
    send_sem, recv_sem = refs[2 * k :]
    n = xs[0].shape[0]
    f = lax.axis_index("feat")
    where = lambda d: (d, f)
    me = _greet("dom", n, where)
    for i in range(k):
        pltpu.make_async_copy(xs[i].at[me], outs[i].at[me], recv_sem.at[i]).start()

    def start(j, carry):
        peer = lax.rem(me + _step(j, n), n)
        for i in range(k):
            pltpu.make_async_remote_copy(
                xs[i].at[peer],
                outs[i].at[me],
                send_sem.at[i],
                recv_sem.at[i],
                device_id=where(peer),
                device_id_type=MESH,
            ).start()
        return carry

    lax.fori_loop(1, n, start, 0)
    for i in range(k):
        sent = xs[i].at[pl.ds(0, n - 1)]
        pltpu.make_async_copy(sent, sent, send_sem.at[i]).wait()
        pltpu.make_async_copy(outs[i], outs[i], recv_sem.at[i]).wait()


def _all_to_all(arrays, cid):
    k = len(arrays)
    return pl.pallas_call(
        _a2a_kernel,
        out_shape=[jax.ShapeDtypeStruct(a.shape, a.dtype) for a in arrays],
        in_specs=[pl.BlockSpec(memory_space=pl.ANY)] * k,
        out_specs=[pl.BlockSpec(memory_space=pl.ANY)] * k,
        scratch_shapes=[
            pltpu.SemaphoreType.DMA((k,)),
            pltpu.SemaphoreType.DMA((k,)),
        ],
        compiler_params=pltpu.CompilerParams(has_side_effects=True, collective_id=cid),
    )(*arrays)


def _gather_kernel(x_ref, o_ref, send_sem, recv_sem, local_sem):
    g = o_ref.shape[0]
    d = lax.axis_index("dom")
    where = lambda q: (d, q)
    me = _greet("feat", g, where)
    local = pltpu.make_async_copy(x_ref, o_ref.at[me], local_sem)
    local.start()

    def copy(peer, slot, s_idx):
        return pltpu.make_async_remote_copy(
            x_ref,
            o_ref.at[slot],
            send_sem.at[s_idx],
            recv_sem.at[slot],
            device_id=where(peer),
            device_id_type=MESH,
        )

    def start(j, carry):
        peer = lax.rem(me + j, g)
        copy(peer, me, peer).start()
        return carry

    lax.fori_loop(1, g, start, 0)

    def wait(j, carry):
        peer = lax.rem(me + j, g)
        src = lax.rem(me + g - j, g)
        copy(peer, me, peer).wait_send()
        copy(src, src, src).wait_recv()
        return carry

    lax.fori_loop(1, g, wait, 0)
    local.wait()


def _feat_gather(x, g, cid):
    return pl.pallas_call(
        _gather_kernel,
        out_shape=jax.ShapeDtypeStruct((g,) + x.shape, x.dtype),
        in_specs=[pl.BlockSpec(memory_space=pl.ANY)],
        out_specs=pl.BlockSpec(memory_space=pl.ANY),
        scratch_shapes=[
            pltpu.SemaphoreType.DMA((g,)),
            pltpu.SemaphoreType.DMA((g,)),
            pltpu.SemaphoreType.DMA(()),
        ],
        compiler_params=pltpu.CompilerParams(has_side_effects=True, collective_id=cid),
    )(x).reshape((g * x.shape[0],) + x.shape[1:])


def _to_chunks(rows, n):
    width, slots = rows.shape
    group = slots // n
    return rows.reshape(width, n, group).transpose(1, 0, 2).reshape(n, width * group // 128, 128)


def _from_chunks(chunks, width):
    n = chunks.shape[0]
    return chunks.reshape(n, width, -1).transpose(1, 0, 2).reshape(width, -1)


def per_device(n_dom, n_feat, replica_feat, adjacency_tiles, tile_index, route, node_feat, w_self, w_neigh):
    feat_width, slot_count = replica_feat.shape
    tile_side = adjacency_tiles.shape[1]
    block_count = slot_count // tile_side
    node_count = node_feat.shape[1]
    full_feat = lax.all_gather(node_feat, "feat", axis=0, tiled=True)
    stacked = replica_feat.reshape(feat_width, block_count, tile_side)
    picked = jnp.take(stacked, tile_index[1], axis=1)
    product = jnp.einsum(
        "ftj,tij->fti", picked, adjacency_tiles, preferred_element_type=jnp.float32
    )
    one_hot = (tile_index[0][:, None] == jnp.arange(block_count, dtype=jnp.int32)[None, :]).astype(
        jnp.float32
    )
    partial_rows = jnp.einsum("fti,tb->fbi", product, one_hot, precision=lax.Precision.HIGHEST)
    partial_rows = partial_rows.reshape(feat_width, slot_count).astype(jnp.bfloat16)
    got, got_route = _all_to_all(
        [_to_chunks(partial_rows, n_dom), route.reshape(n_dom, 1, slot_count // n_dom)], 0
    )
    received = _from_chunks(got, feat_width)
    arrived = got_route.reshape(slot_count)
    chooser = (arrived[:, None] == jnp.arange(node_count, dtype=jnp.int32)[None, :]).astype(
        jnp.bfloat16
    )
    agg = jnp.dot(received, chooser, preferred_element_type=jnp.float32).astype(jnp.bfloat16)
    contract = (((0,), (0,)), ((), ()))
    offset = lax.axis_index("feat") * feat_width
    full_agg = _feat_gather(agg, n_feat, 1)
    self_cols = lax.dynamic_slice_in_dim(w_self, offset, feat_width, 1)
    neigh_cols = lax.dynamic_slice_in_dim(w_neigh, offset, feat_width, 1)
    preact = lax.dot_general(self_cols, full_feat, contract, preferred_element_type=jnp.float32)
    preact = preact + lax.dot_general(
        neigh_cols, full_agg, contract, preferred_element_type=jnp.float32
    )
    renewed = jnp.maximum(preact, jnp.float32(0.0)).astype(jnp.bfloat16)
    gathered_rows = lax.dot_general(
        renewed, chooser, (((1,), (1,)), ((), ())), preferred_element_type=jnp.float32
    ).astype(jnp.bfloat16)
    (back,) = _all_to_all([_to_chunks(gathered_rows, n_dom)], 2)
    replicas = _from_chunks(back, feat_width)
    return (renewed, replicas)


def solution(mesh):
    in_specs = (
        P("feat", "dom"),
        P("dom", None, None),
        P(None, "dom"),
        P(None, "dom"),
        P("feat", "dom"),
        P(),
        P(),
    )
    out_specs = (P("feat", "dom"), P("feat", "dom"))
    body = functools.partial(per_device, mesh.shape["dom"], mesh.shape["feat"])
    return jax.shard_map(body, mesh=mesh, in_specs=in_specs, out_specs=out_specs, check_vma=False)
```

```python
import functools

import jax
import jax.numpy as jnp
from jax import lax
from jax.experimental import pallas as pl
from jax.experimental.pallas import tpu as pltpu
from jax.sharding import PartitionSpec as P

MESH = pl.DeviceIdType.MESH


def _greet(axis, n, where):
    me = lax.axis_index(axis)
    bar = pltpu.get_barrier_semaphore()

    def sig(k, carry):
        pl.semaphore_signal(bar, 1, device_id=where(lax.rem(me + k, n)), device_id_type=MESH)
        return carry

    lax.fori_loop(1, n, sig, 0)
    pl.semaphore_wait(bar, n - 1)
    return me


def _step(j, n):
    half = (j + 1) // 2
    odd = j % 2
    return half * odd + (n - half) * (1 - odd)


def _a2a_kernel(*refs):
    k = (len(refs) - 2) // 2
    xs, outs = refs[:k], refs[k : 2 * k]
    send_sem, recv_sem = refs[2 * k :]
    n = xs[0].shape[0]
    f = lax.axis_index("feat")
    where = lambda d: (d, f)
    me = _greet("dom", n, where)
    for i in range(k):
        pltpu.make_async_copy(xs[i].at[me], outs[i].at[me], recv_sem.at[i]).start()

    def start(j, carry):
        peer = lax.rem(me + _step(j, n), n)
        for i in range(k):
            pltpu.make_async_remote_copy(
                xs[i].at[peer],
                outs[i].at[me],
                send_sem.at[i],
                recv_sem.at[i],
                device_id=where(peer),
                device_id_type=MESH,
            ).start()
        return carry

    lax.fori_loop(1, n, start, 0)
    for i in range(k):
        sent = xs[i].at[pl.ds(0, n - 1)]
        pltpu.make_async_copy(sent, sent, send_sem.at[i]).wait()
        pltpu.make_async_copy(outs[i], outs[i], recv_sem.at[i]).wait()


def _all_to_all(arrays, cid):
    k = len(arrays)
    return pl.pallas_call(
        _a2a_kernel,
        out_shape=[jax.ShapeDtypeStruct(a.shape, a.dtype) for a in arrays],
        in_specs=[pl.BlockSpec(memory_space=pl.ANY)] * k,
        out_specs=[pl.BlockSpec(memory_space=pl.ANY)] * k,
        scratch_shapes=[
            pltpu.SemaphoreType.DMA((k,)),
            pltpu.SemaphoreType.DMA((k,)),
        ],
        compiler_params=pltpu.CompilerParams(has_side_effects=True, collective_id=cid),
    )(*arrays)


def _gather_kernel(x_ref, o_ref, send_sem, recv_sem, local_sem):
    g = o_ref.shape[0]
    d = lax.axis_index("dom")
    where = lambda q: (d, q)
    me = _greet("feat", g, where)
    local = pltpu.make_async_copy(x_ref, o_ref.at[me], local_sem)
    local.start()

    def copy(peer, slot, s_idx):
        return pltpu.make_async_remote_copy(
            x_ref,
            o_ref.at[slot],
            send_sem.at[s_idx],
            recv_sem.at[slot],
            device_id=where(peer),
            device_id_type=MESH,
        )

    def start(j, carry):
        peer = lax.rem(me + j, g)
        copy(peer, me, peer).start()
        return carry

    lax.fori_loop(1, g, start, 0)

    def wait(j, carry):
        peer = lax.rem(me + j, g)
        src = lax.rem(me + g - j, g)
        copy(peer, me, peer).wait_send()
        copy(src, src, src).wait_recv()
        return carry

    lax.fori_loop(1, g, wait, 0)
    local.wait()


def _feat_gather(x, g, cid):
    return pl.pallas_call(
        _gather_kernel,
        out_shape=jax.ShapeDtypeStruct((g,) + x.shape, x.dtype),
        in_specs=[pl.BlockSpec(memory_space=pl.ANY)],
        out_specs=pl.BlockSpec(memory_space=pl.ANY),
        scratch_shapes=[
            pltpu.SemaphoreType.DMA((g,)),
            pltpu.SemaphoreType.DMA((g,)),
            pltpu.SemaphoreType.DMA(()),
        ],
        compiler_params=pltpu.CompilerParams(has_side_effects=True, collective_id=cid),
    )(x).reshape((g * x.shape[0],) + x.shape[1:])


def per_device(n_dom, n_feat, replica_feat, adjacency_tiles, tile_index, route, node_feat, w_self, w_neigh):
    feat_width, slot_count = replica_feat.shape
    tile_side = adjacency_tiles.shape[1]
    block_count = slot_count // tile_side
    node_count = node_feat.shape[1]
    group = slot_count // n_dom
    full_feat = lax.all_gather(node_feat, "feat", axis=0, tiled=True)
    stacked = replica_feat.reshape(feat_width, block_count, tile_side)
    picked = jnp.take(stacked, tile_index[1], axis=1)
    one_hot = (tile_index[0][:, None] == jnp.arange(block_count, dtype=jnp.int32)[None, :]).astype(
        jnp.float32
    )
    halves = []
    for parity in range(2):
        rows = adjacency_tiles[:, parity::2, :]
        product = jnp.einsum("trj,ftj->trf", rows, picked, preferred_element_type=jnp.float32)
        halves.append(
            jnp.einsum("trf,tb->brf", product, one_hot, precision=lax.Precision.HIGHEST)
        )
    paired = jnp.concatenate(halves, axis=2).astype(jnp.bfloat16)
    send = paired.reshape(n_dom, group // 2, 2 * feat_width)
    got, got_route = _all_to_all([send, route.reshape(n_dom, 1, group)], 0)
    arrived = got_route.reshape(slot_count // 2, 2)
    got = got.reshape(slot_count // 2, 2 * feat_width)
    nodes = jnp.arange(node_count, dtype=jnp.int32)[None, :]
    choosers = [(arrived[:, parity][:, None] == nodes).astype(jnp.bfloat16) for parity in range(2)]
    first = (((0,), (0,)), ((), ()))
    agg = sum(
        lax.dot_general(
            got[:, parity * feat_width : (parity + 1) * feat_width],
            choosers[parity],
            first,
            preferred_element_type=jnp.float32,
        )
        for parity in range(2)
    ).astype(jnp.bfloat16)
    offset = lax.axis_index("feat") * feat_width
    full_agg = _feat_gather(agg, n_feat, 1)
    self_cols = lax.dynamic_slice_in_dim(w_self, offset, feat_width, 1)
    neigh_cols = lax.dynamic_slice_in_dim(w_neigh, offset, feat_width, 1)
    preact = lax.dot_general(self_cols, full_feat, first, preferred_element_type=jnp.float32)
    preact = preact + lax.dot_general(neigh_cols, full_agg, first, preferred_element_type=jnp.float32)
    renewed = jnp.maximum(preact, jnp.float32(0.0)).astype(jnp.bfloat16)
    picked_rows = [
        lax.dot_general(
            choosers[parity], renewed, (((1,), (1,)), ((), ())), preferred_element_type=jnp.float32
        ).astype(jnp.bfloat16)
        for parity in range(2)
    ]
    back_send = jnp.concatenate(picked_rows, axis=1).reshape(n_dom, group // 2, 2 * feat_width)
    (back,) = _all_to_all([back_send], 2)
    replicas = back.reshape(n_dom, group // 2, 2, feat_width).transpose(3, 0, 1, 2)
    return (renewed, replicas.reshape(feat_width, slot_count))


def solution(mesh):
    in_specs = (
        P("feat", "dom"),
        P("dom", None, None),
        P(None, "dom"),
        P(None, "dom"),
        P("feat", "dom"),
        P(),
        P(),
    )
    out_specs = (P("feat", "dom"), P("feat", "dom"))
    body = functools.partial(per_device, mesh.shape["dom"], mesh.shape["feat"])
    return jax.shard_map(body, mesh=mesh, in_specs=in_specs, out_specs=out_specs, check_vma=False)
```

```python
import functools

import jax
import jax.numpy as jnp
from jax import lax
from jax.experimental import pallas as pl
from jax.experimental.pallas import tpu as pltpu
from jax.sharding import PartitionSpec as P

MESH = pl.DeviceIdType.MESH


def _greet(axis, n, where):
    me = lax.axis_index(axis)
    bar = pltpu.get_barrier_semaphore()

    def sig(k, carry):
        pl.semaphore_signal(bar, 1, device_id=where(lax.rem(me + k, n)), device_id_type=MESH)
        return carry

    lax.fori_loop(1, n, sig, 0)
    pl.semaphore_wait(bar, n - 1)
    return me


def _step(j, n):
    half = (j + 1) // 2
    odd = j % 2
    return half * odd + (n - half) * (1 - odd)


def _a2a_kernel(*refs):
    k = (len(refs) - 2) // 2
    xs, outs = refs[:k], refs[k : 2 * k]
    send_sem, recv_sem = refs[2 * k :]
    n = xs[0].shape[0]
    f = lax.axis_index("feat")
    where = lambda d: (d, f)
    me = _greet("dom", n, where)
    for i in range(k):
        pltpu.make_async_copy(xs[i].at[me], outs[i].at[me], recv_sem.at[i]).start()

    def start(j, carry):
        peer = lax.rem(me + _step(j, n), n)
        for i in range(k):
            pltpu.make_async_remote_copy(
                xs[i].at[peer],
                outs[i].at[me],
                send_sem.at[i],
                recv_sem.at[i],
                device_id=where(peer),
                device_id_type=MESH,
            ).start()
        return carry

    lax.fori_loop(1, n, start, 0)
    for i in range(k):
        sent = xs[i].at[pl.ds(0, n - 1)]
        pltpu.make_async_copy(sent, sent, send_sem.at[i]).wait()
        pltpu.make_async_copy(outs[i], outs[i], recv_sem.at[i]).wait()


def _all_to_all(arrays, cid):
    k = len(arrays)
    return pl.pallas_call(
        _a2a_kernel,
        out_shape=[jax.ShapeDtypeStruct(a.shape, a.dtype) for a in arrays],
        in_specs=[pl.BlockSpec(memory_space=pl.ANY)] * k,
        out_specs=[pl.BlockSpec(memory_space=pl.ANY)] * k,
        scratch_shapes=[
            pltpu.SemaphoreType.DMA((k,)),
            pltpu.SemaphoreType.DMA((k,)),
        ],
        compiler_params=pltpu.CompilerParams(has_side_effects=True, collective_id=cid),
    )(*arrays)


def _gather_kernel(x_ref, o_ref, send_sem, recv_sem, local_sem):
    g = o_ref.shape[0]
    d = lax.axis_index("dom")
    where = lambda q: (d, q)
    me = _greet("feat", g, where)
    local = pltpu.make_async_copy(x_ref, o_ref.at[me], local_sem)
    local.start()

    def copy(peer, slot, s_idx):
        return pltpu.make_async_remote_copy(
            x_ref,
            o_ref.at[slot],
            send_sem.at[s_idx],
            recv_sem.at[slot],
            device_id=where(peer),
            device_id_type=MESH,
        )

    def start(j, carry):
        peer = lax.rem(me + j, g)
        copy(peer, me, peer).start()
        return carry

    lax.fori_loop(1, g, start, 0)

    def wait(j, carry):
        peer = lax.rem(me + j, g)
        src = lax.rem(me + g - j, g)
        copy(peer, me, peer).wait_send()
        copy(src, src, src).wait_recv()
        return carry

    lax.fori_loop(1, g, wait, 0)
    local.wait()


def _feat_gather(x, g, cid):
    return pl.pallas_call(
        _gather_kernel,
        out_shape=jax.ShapeDtypeStruct((g,) + x.shape, x.dtype),
        in_specs=[pl.BlockSpec(memory_space=pl.ANY)],
        out_specs=pl.BlockSpec(memory_space=pl.ANY),
        scratch_shapes=[
            pltpu.SemaphoreType.DMA((g,)),
            pltpu.SemaphoreType.DMA((g,)),
            pltpu.SemaphoreType.DMA(()),
        ],
        compiler_params=pltpu.CompilerParams(has_side_effects=True, collective_id=cid),
    )(x).reshape((g * x.shape[0],) + x.shape[1:])


def per_device(n_dom, n_feat, replica_feat, adjacency_tiles, tile_index, route, node_feat, w_self, w_neigh):
    feat_width, slot_count = replica_feat.shape
    tile_side = adjacency_tiles.shape[1]
    block_count = slot_count // tile_side
    node_count = node_feat.shape[1]
    group = slot_count // n_dom
    full_feat = lax.all_gather(node_feat, "feat", axis=0, tiled=True)
    stacked = replica_feat.reshape(feat_width, block_count, tile_side)
    picked = jnp.take(stacked, tile_index[1], axis=1)
    one_hot = (tile_index[0][:, None] == jnp.arange(block_count, dtype=jnp.int32)[None, :]).astype(
        jnp.float32
    )
    product = jnp.einsum(
        "tij,ftj->tif", adjacency_tiles, picked, preferred_element_type=jnp.float32
    )
    summed = jnp.einsum("tif,tb->bif", product, one_hot, precision=lax.Precision.HIGHEST)
    paired = summed.astype(jnp.bfloat16)
    send = paired.reshape(n_dom, group // 2, 2 * feat_width)
    got, got_route = _all_to_all([send, route.reshape(n_dom, 1, group)], 0)
    arrived = got_route.reshape(slot_count // 2, 2)
    got = got.reshape(slot_count // 2, 2 * feat_width)
    nodes = jnp.arange(node_count, dtype=jnp.int32)[None, :]
    choosers = [(arrived[:, parity][:, None] == nodes).astype(jnp.bfloat16) for parity in range(2)]
    first = (((0,), (0,)), ((), ()))
    agg = sum(
        lax.dot_general(
            got[:, parity * feat_width : (parity + 1) * feat_width],
            choosers[parity],
            first,
            preferred_element_type=jnp.float32,
        )
        for parity in range(2)
    ).astype(jnp.bfloat16)
    offset = lax.axis_index("feat") * feat_width
    full_agg = _feat_gather(agg, n_feat, 1)
    self_cols = lax.dynamic_slice_in_dim(w_self, offset, feat_width, 1)
    neigh_cols = lax.dynamic_slice_in_dim(w_neigh, offset, feat_width, 1)
    preact = lax.dot_general(self_cols, full_feat, first, preferred_element_type=jnp.float32)
    preact = preact + lax.dot_general(neigh_cols, full_agg, first, preferred_element_type=jnp.float32)
    renewed = jnp.maximum(preact, jnp.float32(0.0)).astype(jnp.bfloat16)
    picked_rows = [
        lax.dot_general(
            choosers[parity], renewed, (((1,), (1,)), ((), ())), preferred_element_type=jnp.float32
        ).astype(jnp.bfloat16)
        for parity in range(2)
    ]
    back_send = jnp.concatenate(picked_rows, axis=1).reshape(n_dom, group // 2, 2 * feat_width)
    (back,) = _all_to_all([back_send], 2)
    replicas = back.reshape(n_dom, group // 2, 2, feat_width).transpose(3, 0, 1, 2)
    return (renewed, replicas.reshape(feat_width, slot_count))


def solution(mesh):
    in_specs = (
        P("feat", "dom"),
        P("dom", None, None),
        P(None, "dom"),
        P(None, "dom"),
        P("feat", "dom"),
        P(),
        P(),
    )
    out_specs = (P("feat", "dom"), P("feat", "dom"))
    body = functools.partial(per_device, mesh.shape["dom"], mesh.shape["feat"])
    return jax.shard_map(body, mesh=mesh, in_specs=in_specs, out_specs=out_specs, check_vma=False)
```

```python
import functools

import jax
import jax.numpy as jnp
from jax import lax
from jax.experimental import pallas as pl
from jax.experimental.pallas import tpu as pltpu
from jax.sharding import PartitionSpec as P

MESH = pl.DeviceIdType.MESH


def _greet(axis, n, where):
    me = lax.axis_index(axis)
    bar = pltpu.get_barrier_semaphore()

    def sig(k, carry):
        pl.semaphore_signal(bar, 1, device_id=where(lax.rem(me + k, n)), device_id_type=MESH)
        return carry

    lax.fori_loop(1, n, sig, 0)
    pl.semaphore_wait(bar, n - 1)
    return me


def _step(j, n):
    half = (j + 1) // 2
    odd = j % 2
    return half * odd + (n - half) * (1 - odd)


def _a2a_kernel(*refs):
    k = (len(refs) - 2) // 2
    xs, outs = refs[:k], refs[k : 2 * k]
    send_sem, recv_sem = refs[2 * k :]
    n = xs[0].shape[0]
    f = lax.axis_index("feat")
    where = lambda d: (d, f)
    me = _greet("dom", n, where)
    for i in range(k):
        pltpu.make_async_copy(xs[i].at[me], outs[i].at[me], recv_sem.at[i]).start()

    def start(j, carry):
        peer = lax.rem(me + _step(j, n), n)
        for i in range(k):
            pltpu.make_async_remote_copy(
                xs[i].at[peer],
                outs[i].at[me],
                send_sem.at[i],
                recv_sem.at[i],
                device_id=where(peer),
                device_id_type=MESH,
            ).start()
        return carry

    lax.fori_loop(1, n, start, 0)
    for i in range(k):
        sent = xs[i].at[pl.ds(0, n - 1)]
        pltpu.make_async_copy(sent, sent, send_sem.at[i]).wait()
        pltpu.make_async_copy(outs[i], outs[i], recv_sem.at[i]).wait()


def _all_to_all(arrays, cid):
    k = len(arrays)
    return pl.pallas_call(
        _a2a_kernel,
        out_shape=[jax.ShapeDtypeStruct(a.shape, a.dtype) for a in arrays],
        in_specs=[pl.BlockSpec(memory_space=pl.ANY)] * k,
        out_specs=[pl.BlockSpec(memory_space=pl.ANY)] * k,
        scratch_shapes=[
            pltpu.SemaphoreType.DMA((k,)),
            pltpu.SemaphoreType.DMA((k,)),
        ],
        compiler_params=pltpu.CompilerParams(has_side_effects=True, collective_id=cid),
    )(*arrays)


def _gather_kernel(x_ref, o_ref, send_sem, recv_sem, local_sem):
    g = o_ref.shape[0]
    d = lax.axis_index("dom")
    where = lambda q: (d, q)
    me = _greet("feat", g, where)
    local = pltpu.make_async_copy(x_ref, o_ref.at[me], local_sem)
    local.start()

    def copy(peer, slot, s_idx):
        return pltpu.make_async_remote_copy(
            x_ref,
            o_ref.at[slot],
            send_sem.at[s_idx],
            recv_sem.at[slot],
            device_id=where(peer),
            device_id_type=MESH,
        )

    def start(j, carry):
        peer = lax.rem(me + j, g)
        copy(peer, me, peer).start()
        return carry

    lax.fori_loop(1, g, start, 0)

    def wait(j, carry):
        peer = lax.rem(me + j, g)
        src = lax.rem(me + g - j, g)
        copy(peer, me, peer).wait_send()
        copy(src, src, src).wait_recv()
        return carry

    lax.fori_loop(1, g, wait, 0)
    local.wait()


def _feat_gather(x, g, cid):
    return pl.pallas_call(
        _gather_kernel,
        out_shape=jax.ShapeDtypeStruct((g,) + x.shape, x.dtype),
        in_specs=[pl.BlockSpec(memory_space=pl.ANY)],
        out_specs=pl.BlockSpec(memory_space=pl.ANY),
        scratch_shapes=[
            pltpu.SemaphoreType.DMA((g,)),
            pltpu.SemaphoreType.DMA((g,)),
            pltpu.SemaphoreType.DMA(()),
        ],
        compiler_params=pltpu.CompilerParams(has_side_effects=True, collective_id=cid),
    )(x).reshape((g * x.shape[0],) + x.shape[1:])


def per_device(n_dom, n_feat, replica_feat, adjacency_tiles, tile_index, route, node_feat, w_self, w_neigh):
    feat_width, slot_count = replica_feat.shape
    tile_side = adjacency_tiles.shape[1]
    block_count = slot_count // tile_side
    node_count = node_feat.shape[1]
    group = slot_count // n_dom
    every_route = lax.all_gather(route, "dom", axis=0, tiled=True)
    full_feat = lax.all_gather(node_feat, "feat", axis=0, tiled=True)
    stacked = replica_feat.reshape(feat_width, block_count, tile_side)
    picked = jnp.take(stacked, tile_index[1], axis=1)
    one_hot = (tile_index[0][:, None] == jnp.arange(block_count, dtype=jnp.int32)[None, :]).astype(
        jnp.float32
    )
    product = jnp.einsum(
        "tij,ftj->tif", adjacency_tiles, picked, preferred_element_type=jnp.float32
    )
    summed = jnp.einsum("tif,tb->bif", product, one_hot, precision=lax.Precision.HIGHEST)
    paired = summed.astype(jnp.bfloat16)
    send = paired.reshape(n_dom, group // 2, 2 * feat_width)
    (got,) = _all_to_all([send], 0)
    arrived = lax.dynamic_slice_in_dim(
        every_route.reshape(n_dom, n_dom, group), lax.axis_index("dom"), 1, 1
    ).reshape(slot_count // 2, 2)
    got = got.reshape(slot_count // 2, 2 * feat_width)
    nodes = jnp.arange(node_count, dtype=jnp.int32)[None, :]
    choosers = [(arrived[:, parity][:, None] == nodes).astype(jnp.bfloat16) for parity in range(2)]
    first = (((0,), (0,)), ((), ()))
    agg = sum(
        lax.dot_general(
            got[:, parity * feat_width : (parity + 1) * feat_width],
            choosers[parity],
            first,
            preferred_element_type=jnp.float32,
        )
        for parity in range(2)
    ).astype(jnp.bfloat16)
    offset = lax.axis_index("feat") * feat_width
    full_agg = _feat_gather(agg, n_feat, 1)
    self_cols = lax.dynamic_slice_in_dim(w_self, offset, feat_width, 1)
    neigh_cols = lax.dynamic_slice_in_dim(w_neigh, offset, feat_width, 1)
    preact = lax.dot_general(self_cols, full_feat, first, preferred_element_type=jnp.float32)
    preact = preact + lax.dot_general(neigh_cols, full_agg, first, preferred_element_type=jnp.float32)
    renewed = jnp.maximum(preact, jnp.float32(0.0)).astype(jnp.bfloat16)
    picked_rows = [
        lax.dot_general(
            choosers[parity], renewed, (((1,), (1,)), ((), ())), preferred_element_type=jnp.float32
        ).astype(jnp.bfloat16)
        for parity in range(2)
    ]
    back_send = jnp.concatenate(picked_rows, axis=1).reshape(n_dom, group // 2, 2 * feat_width)
    (back,) = _all_to_all([back_send], 2)
    replicas = back.reshape(n_dom, group // 2, 2, feat_width).transpose(3, 0, 1, 2)
    return (renewed, replicas.reshape(feat_width, slot_count))


def solution(mesh):
    in_specs = (
        P("feat", "dom"),
        P("dom", None, None),
        P(None, "dom"),
        P(None, "dom"),
        P("feat", "dom"),
        P(),
        P(),
    )
    out_specs = (P("feat", "dom"), P("feat", "dom"))
    body = functools.partial(per_device, mesh.shape["dom"], mesh.shape["feat"])
    return jax.shard_map(body, mesh=mesh, in_specs=in_specs, out_specs=out_specs, check_vma=False)
```

```python
import functools

import jax
import jax.numpy as jnp
from jax import lax
from jax.experimental import pallas as pl
from jax.experimental.pallas import tpu as pltpu
from jax.sharding import PartitionSpec as P

MESH = pl.DeviceIdType.MESH


def _greet(axis, n, where):
    me = lax.axis_index(axis)
    bar = pltpu.get_barrier_semaphore()

    def sig(k, carry):
        pl.semaphore_signal(bar, 1, device_id=where(lax.rem(me + k, n)), device_id_type=MESH)
        return carry

    lax.fori_loop(1, n, sig, 0)
    pl.semaphore_wait(bar, n - 1)
    return me


def _step(j, n):
    half = (j + 1) // 2
    odd = j % 2
    return half * odd + (n - half) * (1 - odd)


def _a2a_kernel(*refs):
    k = (len(refs) - 2) // 2
    xs, outs = refs[:k], refs[k : 2 * k]
    send_sem, recv_sem = refs[2 * k :]
    n = xs[0].shape[0]
    f = lax.axis_index("feat")
    where = lambda d: (d, f)
    me = _greet("dom", n, where)
    for i in range(k):
        pltpu.make_async_copy(xs[i].at[me], outs[i].at[me], recv_sem.at[i]).start()

    def start(j, carry):
        peer = lax.rem(me + _step(j, n), n)
        for i in range(k):
            pltpu.make_async_remote_copy(
                xs[i].at[peer],
                outs[i].at[me],
                send_sem.at[i],
                recv_sem.at[i],
                device_id=where(peer),
                device_id_type=MESH,
            ).start()
        return carry

    lax.fori_loop(1, n, start, 0)
    for i in range(k):
        sent = xs[i].at[pl.ds(0, n - 1)]
        pltpu.make_async_copy(sent, sent, send_sem.at[i]).wait()
        pltpu.make_async_copy(outs[i], outs[i], recv_sem.at[i]).wait()


def _all_to_all(arrays, cid):
    k = len(arrays)
    return pl.pallas_call(
        _a2a_kernel,
        out_shape=[jax.ShapeDtypeStruct(a.shape, a.dtype) for a in arrays],
        in_specs=[pl.BlockSpec(memory_space=pl.ANY)] * k,
        out_specs=[pl.BlockSpec(memory_space=pl.ANY)] * k,
        scratch_shapes=[
            pltpu.SemaphoreType.DMA((k,)),
            pltpu.SemaphoreType.DMA((k,)),
        ],
        compiler_params=pltpu.CompilerParams(has_side_effects=True, collective_id=cid),
    )(*arrays)


def _gather_kernel(x_ref, o_ref, send_sem, recv_sem):
    g = o_ref.shape[0]
    d = lax.axis_index("dom")
    where = lambda q: (d, q)
    me = _greet("feat", g, where)
    pltpu.make_async_copy(x_ref, o_ref.at[me], recv_sem).start()

    def start(j, carry):
        peer = lax.rem(me + j, g)
        pltpu.make_async_remote_copy(
            x_ref, o_ref.at[me], send_sem, recv_sem, device_id=where(peer), device_id_type=MESH
        ).start()
        return carry

    lax.fori_loop(1, g, start, 0)
    sent = o_ref.at[pl.ds(0, g - 1)]
    pltpu.make_async_copy(sent, sent, send_sem).wait()
    pltpu.make_async_copy(o_ref, o_ref, recv_sem).wait()


def _feat_gather(x, g, cid):
    return pl.pallas_call(
        _gather_kernel,
        out_shape=jax.ShapeDtypeStruct((g,) + x.shape, x.dtype),
        in_specs=[pl.BlockSpec(memory_space=pl.ANY)],
        out_specs=pl.BlockSpec(memory_space=pl.ANY),
        scratch_shapes=[pltpu.SemaphoreType.DMA(()), pltpu.SemaphoreType.DMA(())],
        compiler_params=pltpu.CompilerParams(has_side_effects=True, collective_id=cid),
    )(x).reshape((g * x.shape[0],) + x.shape[1:])


def per_device(n_dom, n_feat, replica_feat, adjacency_tiles, tile_index, route, node_feat, w_self, w_neigh):
    feat_width, slot_count = replica_feat.shape
    tile_side = adjacency_tiles.shape[1]
    block_count = slot_count // tile_side
    node_count = node_feat.shape[1]
    group = slot_count // n_dom
    full_feat = lax.all_gather(node_feat, "feat", axis=0, tiled=True)
    stacked = replica_feat.reshape(feat_width, block_count, tile_side)
    picked = jnp.take(stacked, tile_index[1], axis=1)
    one_hot = (tile_index[0][:, None] == jnp.arange(block_count, dtype=jnp.int32)[None, :]).astype(
        jnp.float32
    )
    product = jnp.einsum(
        "tij,ftj->tif", adjacency_tiles, picked, preferred_element_type=jnp.float32
    )
    summed = jnp.einsum("tif,tb->bif", product, one_hot, precision=lax.Precision.HIGH)
    paired = summed.astype(jnp.bfloat16)
    send = paired.reshape(n_dom, group // 2, 2 * feat_width)
    got, got_route = _all_to_all([send, route.reshape(n_dom, 1, group)], 0)
    arrived = got_route.reshape(slot_count // 2, 2)
    got = got.reshape(slot_count // 2, 2 * feat_width)
    nodes = jnp.arange(node_count, dtype=jnp.int32)[None, :]
    choosers = [(arrived[:, parity][:, None] == nodes).astype(jnp.bfloat16) for parity in range(2)]
    first = (((0,), (0,)), ((), ()))
    agg = sum(
        lax.dot_general(
            got[:, parity * feat_width : (parity + 1) * feat_width],
            choosers[parity],
            first,
            preferred_element_type=jnp.float32,
        )
        for parity in range(2)
    ).astype(jnp.bfloat16)
    offset = lax.axis_index("feat") * feat_width
    full_agg = _feat_gather(agg, n_feat, 1)
    self_cols = lax.dynamic_slice_in_dim(w_self, offset, feat_width, 1)
    neigh_cols = lax.dynamic_slice_in_dim(w_neigh, offset, feat_width, 1)
    preact = lax.dot_general(self_cols, full_feat, first, preferred_element_type=jnp.float32)
    preact = preact + lax.dot_general(neigh_cols, full_agg, first, preferred_element_type=jnp.float32)
    renewed = jnp.maximum(preact, jnp.float32(0.0)).astype(jnp.bfloat16)
    picked_rows = [
        lax.dot_general(
            choosers[parity], renewed, (((1,), (1,)), ((), ())), preferred_element_type=jnp.float32
        ).astype(jnp.bfloat16)
        for parity in range(2)
    ]
    back_send = jnp.concatenate(picked_rows, axis=1).reshape(n_dom, group // 2, 2 * feat_width)
    (back,) = _all_to_all([back_send], 2)
    replicas = back.reshape(n_dom, group // 2, 2, feat_width).transpose(3, 0, 1, 2)
    return (renewed, replicas.reshape(feat_width, slot_count))


def solution(mesh):
    in_specs = (
        P("feat", "dom"),
        P("dom", None, None),
        P(None, "dom"),
        P(None, "dom"),
        P("feat", "dom"),
        P(),
        P(),
    )
    out_specs = (P("feat", "dom"), P("feat", "dom"))
    body = functools.partial(per_device, mesh.shape["dom"], mesh.shape["feat"])
    return jax.shard_map(body, mesh=mesh, in_specs=in_specs, out_specs=out_specs, check_vma=False)
```

```python
import functools

import jax
import jax.numpy as jnp
from jax import lax
from jax.experimental import pallas as pl
from jax.experimental.pallas import tpu as pltpu
from jax.sharding import PartitionSpec as P

MESH = pl.DeviceIdType.MESH


def _greet(axis, n, where):
    me = lax.axis_index(axis)
    bar = pltpu.get_barrier_semaphore()

    def sig(k, carry):
        pl.semaphore_signal(bar, 1, device_id=where(lax.rem(me + k, n)), device_id_type=MESH)
        return carry

    lax.fori_loop(1, n, sig, 0)
    pl.semaphore_wait(bar, n - 1)
    return me


def _step(j, n):
    half = (j + 1) // 2
    odd = j % 2
    return half * odd + (n - half) * (1 - odd)


def _a2a_kernel(*refs):
    k = (len(refs) - 2) // 2
    xs, outs = refs[:k], refs[k : 2 * k]
    send_sem, recv_sem = refs[2 * k :]
    n = xs[0].shape[0]
    f = lax.axis_index("feat")
    where = lambda d: (d, f)
    me = _greet("dom", n, where)
    for i in range(k):
        pltpu.make_async_copy(xs[i].at[me], outs[i].at[me], recv_sem.at[i]).start()

    def start(j, carry):
        peer = lax.rem(me + _step(j, n), n)
        for i in range(k):
            pltpu.make_async_remote_copy(
                xs[i].at[peer],
                outs[i].at[me],
                send_sem.at[i],
                recv_sem.at[i],
                device_id=where(peer),
                device_id_type=MESH,
            ).start()
        return carry

    lax.fori_loop(1, n, start, 0)
    for i in range(k):
        sent = xs[i].at[pl.ds(0, n - 1)]
        pltpu.make_async_copy(sent, sent, send_sem.at[i]).wait()
        pltpu.make_async_copy(outs[i], outs[i], recv_sem.at[i]).wait()


def _all_to_all(arrays, cid):
    k = len(arrays)
    return pl.pallas_call(
        _a2a_kernel,
        out_shape=[jax.ShapeDtypeStruct(a.shape, a.dtype) for a in arrays],
        in_specs=[pl.BlockSpec(memory_space=pl.ANY)] * k,
        out_specs=[pl.BlockSpec(memory_space=pl.ANY)] * k,
        scratch_shapes=[
            pltpu.SemaphoreType.DMA((k,)),
            pltpu.SemaphoreType.DMA((k,)),
        ],
        compiler_params=pltpu.CompilerParams(has_side_effects=True, collective_id=cid),
    )(*arrays)


def _gather_kernel(x_ref, o_ref, send_sem, recv_sem):
    g = o_ref.shape[0]
    d = lax.axis_index("dom")
    where = lambda q: (d, q)
    me = _greet("feat", g, where)
    pltpu.make_async_copy(x_ref, o_ref.at[me], recv_sem).start()

    def start(j, carry):
        peer = lax.rem(me + j, g)
        pltpu.make_async_remote_copy(
            x_ref, o_ref.at[me], send_sem, recv_sem, device_id=where(peer), device_id_type=MESH
        ).start()
        return carry

    lax.fori_loop(1, g, start, 0)
    sent = o_ref.at[pl.ds(0, g - 1)]
    pltpu.make_async_copy(sent, sent, send_sem).wait()
    pltpu.make_async_copy(o_ref, o_ref, recv_sem).wait()


def _feat_gather(x, g, cid):
    return pl.pallas_call(
        _gather_kernel,
        out_shape=jax.ShapeDtypeStruct((g,) + x.shape, x.dtype),
        in_specs=[pl.BlockSpec(memory_space=pl.ANY)],
        out_specs=pl.BlockSpec(memory_space=pl.ANY),
        scratch_shapes=[pltpu.SemaphoreType.DMA(()), pltpu.SemaphoreType.DMA(())],
        compiler_params=pltpu.CompilerParams(has_side_effects=True, collective_id=cid),
    )(x).reshape((g * x.shape[0],) + x.shape[1:])


def per_device(n_dom, n_feat, replica_feat, adjacency_tiles, tile_index, route, node_feat, w_self, w_neigh):
    feat_width, slot_count = replica_feat.shape
    tile_side = adjacency_tiles.shape[1]
    block_count = slot_count // tile_side
    node_count = node_feat.shape[1]
    group = slot_count // n_dom
    full_feat = lax.all_gather(node_feat, "feat", axis=0, tiled=True)
    stacked = replica_feat.reshape(feat_width, block_count, tile_side)
    picked = jnp.take(stacked, tile_index[1], axis=1)
    one_hot = (tile_index[0][:, None] == jnp.arange(block_count, dtype=jnp.int32)[None, :]).astype(
        jnp.float32
    )
    product = jnp.einsum(
        "tij,ftj->tif", adjacency_tiles, picked, preferred_element_type=jnp.float32
    )
    summed = jnp.einsum("tif,tb->bif", product, one_hot, precision=lax.Precision.HIGH)
    paired = summed.astype(jnp.bfloat16)
    send = paired.reshape(n_dom, group // 2, 2 * feat_width)
    half = group // 2
    route_pairs = route.reshape(n_dom, half, 2).transpose(0, 2, 1).reshape(n_dom, 1, group)
    got, got_route = _all_to_all([send, route_pairs], 0)
    got = got.reshape(slot_count // 2, 2 * feat_width)
    got_route = got_route.reshape(n_dom, 2, half)
    nodes = jnp.arange(node_count, dtype=jnp.int32)[:, None]
    choosers = [
        (got_route[:, parity, :].reshape(1, n_dom * half) == nodes).astype(jnp.bfloat16)
        for parity in range(2)
    ]
    first = (((0,), (0,)), ((), ()))
    agg = sum(
        lax.dot_general(
            got[:, parity * feat_width : (parity + 1) * feat_width],
            choosers[parity],
            (((0,), (1,)), ((), ())),
            preferred_element_type=jnp.float32,
        )
        for parity in range(2)
    ).astype(jnp.bfloat16)
    offset = lax.axis_index("feat") * feat_width
    full_agg = _feat_gather(agg, n_feat, 1)
    self_cols = lax.dynamic_slice_in_dim(w_self, offset, feat_width, 1)
    neigh_cols = lax.dynamic_slice_in_dim(w_neigh, offset, feat_width, 1)
    preact = lax.dot_general(self_cols, full_feat, first, preferred_element_type=jnp.float32)
    preact = preact + lax.dot_general(neigh_cols, full_agg, first, preferred_element_type=jnp.float32)
    renewed = jnp.maximum(preact, jnp.float32(0.0)).astype(jnp.bfloat16)
    picked_rows = [
        lax.dot_general(
            choosers[parity], renewed, (((0,), (1,)), ((), ())), preferred_element_type=jnp.float32
        ).astype(jnp.bfloat16)
        for parity in range(2)
    ]
    back_send = jnp.concatenate(picked_rows, axis=1).reshape(n_dom, group // 2, 2 * feat_width)
    (back,) = _all_to_all([back_send], 2)
    replicas = back.reshape(n_dom, group // 2, 2, feat_width).transpose(3, 0, 1, 2)
    return (renewed, replicas.reshape(feat_width, slot_count))


def solution(mesh):
    in_specs = (
        P("feat", "dom"),
        P("dom", None, None),
        P(None, "dom"),
        P(None, "dom"),
        P("feat", "dom"),
        P(),
        P(),
    )
    out_specs = (P("feat", "dom"), P("feat", "dom"))
    body = functools.partial(per_device, mesh.shape["dom"], mesh.shape["feat"])
    return jax.shard_map(body, mesh=mesh, in_specs=in_specs, out_specs=out_specs, check_vma=False)
```

```python
import functools

import jax
import jax.numpy as jnp
from jax import lax
from jax.experimental import pallas as pl
from jax.experimental.pallas import tpu as pltpu
from jax.sharding import PartitionSpec as P

MESH = pl.DeviceIdType.MESH


def _greet(axis, n, where):
    me = lax.axis_index(axis)
    bar = pltpu.get_barrier_semaphore()

    def sig(k, carry):
        pl.semaphore_signal(bar, 1, device_id=where(lax.rem(me + k, n)), device_id_type=MESH)
        return carry

    lax.fori_loop(1, n, sig, 0)
    pl.semaphore_wait(bar, n - 1)
    return me


def _step(j, n):
    half = (j + 1) // 2
    odd = j % 2
    return half * odd + (n - half) * (1 - odd)


def _a2a_kernel(*refs):
    k = (len(refs) - 2) // 2
    xs, outs = refs[:k], refs[k : 2 * k]
    send_sem, recv_sem = refs[2 * k :]
    n = xs[0].shape[0]
    f = lax.axis_index("feat")
    where = lambda d: (d, f)
    me = _greet("dom", n, where)
    for i in range(k):
        pltpu.make_async_copy(xs[i].at[me], outs[i].at[me], recv_sem.at[i]).start()

    def start(j, carry):
        peer = lax.rem(me + _step(j, n), n)
        for i in range(k):
            pltpu.make_async_remote_copy(
                xs[i].at[peer],
                outs[i].at[me],
                send_sem.at[i],
                recv_sem.at[i],
                device_id=where(peer),
                device_id_type=MESH,
            ).start()
        return carry

    lax.fori_loop(1, n, start, 0)
    for i in range(k):
        sent = xs[i].at[pl.ds(0, n - 1)]
        pltpu.make_async_copy(sent, sent, send_sem.at[i]).wait()
        pltpu.make_async_copy(outs[i], outs[i], recv_sem.at[i]).wait()


def _all_to_all(arrays, cid):
    k = len(arrays)
    return pl.pallas_call(
        _a2a_kernel,
        out_shape=[jax.ShapeDtypeStruct(a.shape, a.dtype) for a in arrays],
        in_specs=[pl.BlockSpec(memory_space=pl.ANY)] * k,
        out_specs=[pl.BlockSpec(memory_space=pl.ANY)] * k,
        scratch_shapes=[
            pltpu.SemaphoreType.DMA((k,)),
            pltpu.SemaphoreType.DMA((k,)),
        ],
        compiler_params=pltpu.CompilerParams(has_side_effects=True, collective_id=cid),
    )(*arrays)


def _gather_kernel(x_ref, o_ref, send_sem, recv_sem):
    g = o_ref.shape[0]
    d = lax.axis_index("dom")
    where = lambda q: (d, q)
    me = _greet("feat", g, where)
    right, left, far = lax.rem(me + 1, g), lax.rem(me + g - 1, g), lax.rem(me + 2, g)
    h = o_ref.shape[1] // 2

    def arrived(slot):
        pltpu.make_async_copy(o_ref.at[slot], o_ref.at[slot], recv_sem.at[slot]).wait()

    def send(src, dst, slot, peer):
        pltpu.make_async_remote_copy(
            src, dst, send_sem, recv_sem.at[slot], device_id=where(peer), device_id_type=MESH
        ).start()

    pltpu.make_async_copy(x_ref, o_ref.at[me], recv_sem.at[me]).start()
    send(x_ref, o_ref.at[me], me, right)
    send(x_ref, o_ref.at[me], me, left)
    arrived(left)
    arrived(right)
    send(o_ref.at[left, pl.ds(0, h)], o_ref.at[left, pl.ds(0, h)], left, right)
    send(o_ref.at[right, pl.ds(h, h)], o_ref.at[right, pl.ds(h, h)], right, left)
    arrived(far)
    arrived(me)
    sent = o_ref.at[pl.ds(0, g - 1)]
    pltpu.make_async_copy(sent, sent, send_sem).wait()


def _feat_gather(x, g, cid):
    return pl.pallas_call(
        _gather_kernel,
        out_shape=jax.ShapeDtypeStruct((g,) + x.shape, x.dtype),
        in_specs=[pl.BlockSpec(memory_space=pl.ANY)],
        out_specs=pl.BlockSpec(memory_space=pl.ANY),
        scratch_shapes=[pltpu.SemaphoreType.DMA(()), pltpu.SemaphoreType.DMA((g,))],
        compiler_params=pltpu.CompilerParams(has_side_effects=True, collective_id=cid),
    )(x).reshape((g * x.shape[0],) + x.shape[1:])


def per_device(n_dom, n_feat, replica_feat, adjacency_tiles, tile_index, route, node_feat, w_self, w_neigh):
    feat_width, slot_count = replica_feat.shape
    tile_side = adjacency_tiles.shape[1]
    block_count = slot_count // tile_side
    node_count = node_feat.shape[1]
    group = slot_count // n_dom
    full_feat = lax.all_gather(node_feat, "feat", axis=0, tiled=True)
    stacked = replica_feat.reshape(feat_width, block_count, tile_side)
    picked = jnp.take(stacked, tile_index[1], axis=1)
    one_hot = (tile_index[0][:, None] == jnp.arange(block_count, dtype=jnp.int32)[None, :]).astype(
        jnp.float32
    )
    product = jnp.einsum(
        "tij,ftj->tif", adjacency_tiles, picked, preferred_element_type=jnp.float32
    )
    summed = jnp.einsum("tif,tb->bif", product, one_hot, precision=lax.Precision.HIGH)
    paired = summed.astype(jnp.bfloat16)
    send = paired.reshape(n_dom, group // 2, 2 * feat_width)
    half = group // 2
    route_pairs = route.reshape(n_dom, half, 2).transpose(0, 2, 1).reshape(n_dom, 1, group)
    got, got_route = _all_to_all([send, route_pairs], 0)
    got = got.reshape(slot_count // 2, 2 * feat_width)
    got_route = got_route.reshape(n_dom, 2, half)
    nodes = jnp.arange(node_count, dtype=jnp.int32)[:, None]
    choosers = [
        (got_route[:, parity, :].reshape(1, n_dom * half) == nodes).astype(jnp.bfloat16)
        for parity in range(2)
    ]
    first = (((0,), (0,)), ((), ()))
    agg = sum(
        lax.dot_general(
            got[:, parity * feat_width : (parity + 1) * feat_width],
            choosers[parity],
            (((0,), (1,)), ((), ())),
            preferred_element_type=jnp.float32,
        )
        for parity in range(2)
    ).astype(jnp.bfloat16)
    offset = lax.axis_index("feat") * feat_width
    full_agg = _feat_gather(agg, n_feat, 1)
    self_cols = lax.dynamic_slice_in_dim(w_self, offset, feat_width, 1)
    neigh_cols = lax.dynamic_slice_in_dim(w_neigh, offset, feat_width, 1)
    preact = lax.dot_general(self_cols, full_feat, first, preferred_element_type=jnp.float32)
    preact = preact + lax.dot_general(neigh_cols, full_agg, first, preferred_element_type=jnp.float32)
    renewed = jnp.maximum(preact, jnp.float32(0.0)).astype(jnp.bfloat16)
    picked_rows = [
        lax.dot_general(
            choosers[parity], renewed, (((0,), (1,)), ((), ())), preferred_element_type=jnp.float32
        ).astype(jnp.bfloat16)
        for parity in range(2)
    ]
    back_send = jnp.concatenate(picked_rows, axis=1).reshape(n_dom, group // 2, 2 * feat_width)
    (back,) = _all_to_all([back_send], 2)
    replicas = back.reshape(n_dom, group // 2, 2, feat_width).transpose(3, 0, 1, 2)
    return (renewed, replicas.reshape(feat_width, slot_count))


def solution(mesh):
    in_specs = (
        P("feat", "dom"),
        P("dom", None, None),
        P(None, "dom"),
        P(None, "dom"),
        P("feat", "dom"),
        P(),
        P(),
    )
    out_specs = (P("feat", "dom"), P("feat", "dom"))
    body = functools.partial(per_device, mesh.shape["dom"], mesh.shape["feat"])
    return jax.shard_map(body, mesh=mesh, in_specs=in_specs, out_specs=out_specs, check_vma=False)
```

```python
import functools

import jax
import jax.numpy as jnp
from jax import lax
from jax.experimental import pallas as pl
from jax.experimental.pallas import tpu as pltpu
from jax.sharding import PartitionSpec as P

MESH = pl.DeviceIdType.MESH


def _greet(axis, n, where):
    me = lax.axis_index(axis)
    bar = pltpu.get_barrier_semaphore()

    def sig(k, carry):
        pl.semaphore_signal(bar, 1, device_id=where(lax.rem(me + k, n)), device_id_type=MESH)
        return carry

    lax.fori_loop(1, n, sig, 0)
    pl.semaphore_wait(bar, n - 1)
    return me


def _step(j, n):
    half = (j + 1) // 2
    odd = j % 2
    return half * odd + (n - half) * (1 - odd)


def _a2a_kernel(*refs):
    k = (len(refs) - 2) // 2
    xs, outs = refs[:k], refs[k : 2 * k]
    send_sem, recv_sem = refs[2 * k :]
    n = xs[0].shape[0]
    f = lax.axis_index("feat")
    where = lambda d: (d, f)
    me = _greet("dom", n, where)
    for i in range(k):
        pltpu.make_async_copy(xs[i].at[me], outs[i].at[me], recv_sem.at[i]).start()

    def start(j, carry):
        peer = lax.rem(me + _step(j, n), n)
        for i in range(k):
            pltpu.make_async_remote_copy(
                xs[i].at[peer],
                outs[i].at[me],
                send_sem.at[i],
                recv_sem.at[i],
                device_id=where(peer),
                device_id_type=MESH,
            ).start()
        return carry

    lax.fori_loop(1, n, start, 0)
    for i in range(k):
        sent = xs[i].at[pl.ds(0, n - 1)]
        pltpu.make_async_copy(sent, sent, send_sem.at[i]).wait()
        pltpu.make_async_copy(outs[i], outs[i], recv_sem.at[i]).wait()


def _all_to_all(arrays, cid):
    k = len(arrays)
    return pl.pallas_call(
        _a2a_kernel,
        out_shape=[jax.ShapeDtypeStruct(a.shape, a.dtype) for a in arrays],
        in_specs=[pl.BlockSpec(memory_space=pl.ANY)] * k,
        out_specs=[pl.BlockSpec(memory_space=pl.ANY)] * k,
        scratch_shapes=[
            pltpu.SemaphoreType.DMA((k,)),
            pltpu.SemaphoreType.DMA((k,)),
        ],
        compiler_params=pltpu.CompilerParams(has_side_effects=True, collective_id=cid),
    )(*arrays)


def _gather_kernel(pieces, x_ref, o_ref, send_sem, recv_sem):
    g = o_ref.shape[0]
    d = lax.axis_index("dom")
    where = lambda q: (d, q)
    me = _greet("feat", g, where)
    rows = o_ref.shape[1] // pieces
    pltpu.make_async_copy(x_ref, o_ref.at[me], recv_sem.at[me]).start()
    for j in range(1, g):
        peer = lax.rem(me + j, g)
        for p in range(pieces):
            part = pl.ds(p * rows, rows)
            pltpu.make_async_remote_copy(
                x_ref.at[part],
                o_ref.at[me, part],
                send_sem,
                recv_sem.at[me],
                device_id=where(peer),
                device_id_type=MESH,
            ).start()
    for j in range(g):
        slot = lax.rem(me + j, g)
        pltpu.make_async_copy(o_ref.at[slot], o_ref.at[slot], recv_sem.at[slot]).wait()
    sent = o_ref.at[pl.ds(0, g - 1)]
    pltpu.make_async_copy(sent, sent, send_sem).wait()


def _feat_gather(x, g, cid):
    return pl.pallas_call(
        functools.partial(_gather_kernel, 8),
        out_shape=jax.ShapeDtypeStruct((g,) + x.shape, x.dtype),
        in_specs=[pl.BlockSpec(memory_space=pl.ANY)],
        out_specs=pl.BlockSpec(memory_space=pl.ANY),
        scratch_shapes=[pltpu.SemaphoreType.DMA(()), pltpu.SemaphoreType.DMA((g,))],
        compiler_params=pltpu.CompilerParams(has_side_effects=True, collective_id=cid),
    )(x).reshape((g * x.shape[0],) + x.shape[1:])


def per_device(n_dom, n_feat, replica_feat, adjacency_tiles, tile_index, route, node_feat, w_self, w_neigh):
    feat_width, slot_count = replica_feat.shape
    tile_side = adjacency_tiles.shape[1]
    block_count = slot_count // tile_side
    node_count = node_feat.shape[1]
    group = slot_count // n_dom
    full_feat = lax.all_gather(node_feat, "feat", axis=0, tiled=True)
    stacked = replica_feat.reshape(feat_width, block_count, tile_side)
    picked = jnp.take(stacked, tile_index[1], axis=1)
    one_hot = (tile_index[0][:, None] == jnp.arange(block_count, dtype=jnp.int32)[None, :]).astype(
        jnp.float32
    )
    product = jnp.einsum(
        "tij,ftj->tif", adjacency_tiles, picked, preferred_element_type=jnp.float32
    )
    summed = jnp.einsum("tif,tb->bif", product, one_hot, precision=lax.Precision.HIGH)
    paired = summed.astype(jnp.bfloat16)
    send = paired.reshape(n_dom, group // 2, 2 * feat_width)
    half = group // 2
    route_pairs = route.reshape(n_dom, half, 2).transpose(0, 2, 1).reshape(n_dom, 1, group)
    got, got_route = _all_to_all([send, route_pairs], 0)
    got = got.reshape(slot_count // 2, 2 * feat_width)
    got_route = got_route.reshape(n_dom, 2, half)
    nodes = jnp.arange(node_count, dtype=jnp.int32)[:, None]
    choosers = [
        (got_route[:, parity, :].reshape(1, n_dom * half) == nodes).astype(jnp.bfloat16)
        for parity in range(2)
    ]
    first = (((0,), (0,)), ((), ()))
    agg = sum(
        lax.dot_general(
            got[:, parity * feat_width : (parity + 1) * feat_width],
            choosers[parity],
            (((0,), (1,)), ((), ())),
            preferred_element_type=jnp.float32,
        )
        for parity in range(2)
    ).astype(jnp.bfloat16)
    offset = lax.axis_index("feat") * feat_width
    full_agg = _feat_gather(agg, n_feat, 1)
    self_cols = lax.dynamic_slice_in_dim(w_self, offset, feat_width, 1)
    neigh_cols = lax.dynamic_slice_in_dim(w_neigh, offset, feat_width, 1)
    preact = lax.dot_general(self_cols, full_feat, first, preferred_element_type=jnp.float32)
    preact = preact + lax.dot_general(neigh_cols, full_agg, first, preferred_element_type=jnp.float32)
    renewed = jnp.maximum(preact, jnp.float32(0.0)).astype(jnp.bfloat16)
    picked_rows = [
        lax.dot_general(
            choosers[parity], renewed, (((0,), (1,)), ((), ())), preferred_element_type=jnp.float32
        ).astype(jnp.bfloat16)
        for parity in range(2)
    ]
    back_send = jnp.concatenate(picked_rows, axis=1).reshape(n_dom, group // 2, 2 * feat_width)
    (back,) = _all_to_all([back_send], 2)
    replicas = back.reshape(n_dom, group // 2, 2, feat_width).transpose(3, 0, 1, 2)
    return (renewed, replicas.reshape(feat_width, slot_count))


def solution(mesh):
    in_specs = (
        P("feat", "dom"),
        P("dom", None, None),
        P(None, "dom"),
        P(None, "dom"),
        P("feat", "dom"),
        P(),
        P(),
    )
    out_specs = (P("feat", "dom"), P("feat", "dom"))
    body = functools.partial(per_device, mesh.shape["dom"], mesh.shape["feat"])
    return jax.shard_map(body, mesh=mesh, in_specs=in_specs, out_specs=out_specs, check_vma=False)
```

```python
import functools

import jax
import jax.numpy as jnp
from jax import lax
from jax.experimental import pallas as pl
from jax.experimental.pallas import tpu as pltpu
from jax.sharding import PartitionSpec as P

MESH = pl.DeviceIdType.MESH


def _greet(axis, n, where):
    me = lax.axis_index(axis)
    bar = pltpu.get_barrier_semaphore()

    def sig(k, carry):
        pl.semaphore_signal(bar, 1, device_id=where(lax.rem(me + k, n)), device_id_type=MESH)
        return carry

    lax.fori_loop(1, n, sig, 0, unroll=8)
    pl.semaphore_wait(bar, n - 1)
    return me


def _a2a_kernel(*refs):
    k = (len(refs) - 2) // 2
    xs, outs = refs[:k], refs[k : 2 * k]
    send_sem, recv_sem = refs[2 * k :]
    n = xs[0].shape[0]
    f = lax.axis_index("feat")
    where = lambda d: (d, f)
    me = _greet("dom", n, where)
    for i in range(k):
        pltpu.make_async_copy(xs[i].at[me], outs[i].at[me], recv_sem.at[i]).start()

    def start(j, carry):
        peer = lax.rem(me + j, n)
        for i in range(k):
            pltpu.make_async_remote_copy(
                xs[i].at[peer],
                outs[i].at[me],
                send_sem.at[i],
                recv_sem.at[i],
                device_id=where(peer),
                device_id_type=MESH,
            ).start()
        return carry

    lax.fori_loop(1, n, start, 0, unroll=8)
    for i in range(k):
        sent = xs[i].at[pl.ds(0, n - 1)]
        pltpu.make_async_copy(sent, sent, send_sem.at[i]).wait()
        pltpu.make_async_copy(outs[i], outs[i], recv_sem.at[i]).wait()


def _all_to_all(arrays, cid):
    k = len(arrays)
    return pl.pallas_call(
        _a2a_kernel,
        out_shape=[jax.ShapeDtypeStruct(a.shape, a.dtype) for a in arrays],
        in_specs=[pl.BlockSpec(memory_space=pl.ANY)] * k,
        out_specs=[pl.BlockSpec(memory_space=pl.ANY)] * k,
        scratch_shapes=[
            pltpu.SemaphoreType.DMA((k,)),
            pltpu.SemaphoreType.DMA((k,)),
        ],
        compiler_params=pltpu.CompilerParams(has_side_effects=True, collective_id=cid),
    )(*arrays)


def _gather_kernel(x_ref, o_ref, send_sem, recv_sem):
    g = o_ref.shape[0]
    d = lax.axis_index("dom")
    where = lambda q: (d, q)
    me = _greet("feat", g, where)
    right, left, far = lax.rem(me + 1, g), lax.rem(me + g - 1, g), lax.rem(me + 2, g)
    h = o_ref.shape[1] // 2

    def arrived(slot):
        pltpu.make_async_copy(o_ref.at[slot], o_ref.at[slot], recv_sem.at[slot]).wait()

    def send(src, dst, slot, peer):
        pltpu.make_async_remote_copy(
            src, dst, send_sem, recv_sem.at[slot], device_id=where(peer), device_id_type=MESH
        ).start()

    pltpu.make_async_copy(x_ref, o_ref.at[me], recv_sem.at[me]).start()
    send(x_ref, o_ref.at[me], me, right)
    send(x_ref, o_ref.at[me], me, left)
    arrived(left)
    arrived(right)
    send(o_ref.at[left, pl.ds(0, h)], o_ref.at[left, pl.ds(0, h)], left, right)
    send(o_ref.at[right, pl.ds(h, h)], o_ref.at[right, pl.ds(h, h)], right, left)
    arrived(far)
    arrived(me)
    sent = o_ref.at[pl.ds(0, g - 1)]
    pltpu.make_async_copy(sent, sent, send_sem).wait()


def _feat_gather(x, g, cid):
    return pl.pallas_call(
        _gather_kernel,
        out_shape=jax.ShapeDtypeStruct((g,) + x.shape, x.dtype),
        in_specs=[pl.BlockSpec(memory_space=pl.ANY)],
        out_specs=pl.BlockSpec(memory_space=pl.ANY),
        scratch_shapes=[pltpu.SemaphoreType.DMA(()), pltpu.SemaphoreType.DMA((g,))],
        compiler_params=pltpu.CompilerParams(has_side_effects=True, collective_id=cid),
    )(x).reshape((g * x.shape[0],) + x.shape[1:])


def per_device(n_dom, n_feat, replica_feat, adjacency_tiles, tile_index, route, node_feat, w_self, w_neigh):
    feat_width, slot_count = replica_feat.shape
    tile_side = adjacency_tiles.shape[1]
    block_count = slot_count // tile_side
    node_count = node_feat.shape[1]
    group = slot_count // n_dom
    full_feat = lax.all_gather(node_feat, "feat", axis=0, tiled=True)
    stacked = replica_feat.reshape(feat_width, block_count, tile_side)
    picked = jnp.take(stacked, tile_index[1], axis=1)
    one_hot = (tile_index[0][:, None] == jnp.arange(block_count, dtype=jnp.int32)[None, :]).astype(
        jnp.float32
    )
    product = jnp.einsum(
        "tij,ftj->tif", adjacency_tiles, picked, preferred_element_type=jnp.float32
    )
    summed = jnp.einsum("tif,tb->bif", product, one_hot, precision=lax.Precision.HIGH)
    paired = summed.astype(jnp.bfloat16)
    send = paired.reshape(n_dom, group // 2, 2 * feat_width)
    half = group // 2
    route_pairs = route.reshape(n_dom, half, 2).transpose(0, 2, 1).reshape(n_dom, 1, group)
    got, got_route = _all_to_all([send, route_pairs], 0)
    got = got.reshape(slot_count // 2, 2 * feat_width)
    got_route = got_route.reshape(n_dom, 2, half)
    nodes = jnp.arange(node_count, dtype=jnp.int32)[:, None]
    choosers = [
        (got_route[:, parity, :].reshape(1, n_dom * half) == nodes).astype(jnp.bfloat16)
        for parity in range(2)
    ]
    first = (((0,), (0,)), ((), ()))
    agg = sum(
        lax.dot_general(
            got[:, parity * feat_width : (parity + 1) * feat_width],
            choosers[parity],
            (((0,), (1,)), ((), ())),
            preferred_element_type=jnp.float32,
        )
        for parity in range(2)
    ).astype(jnp.bfloat16)
    offset = lax.axis_index("feat") * feat_width
    full_agg = _feat_gather(agg, n_feat, 1)
    self_cols = lax.dynamic_slice_in_dim(w_self, offset, feat_width, 1)
    neigh_cols = lax.dynamic_slice_in_dim(w_neigh, offset, feat_width, 1)
    preact = lax.dot_general(self_cols, full_feat, first, preferred_element_type=jnp.float32)
    preact = preact + lax.dot_general(neigh_cols, full_agg, first, preferred_element_type=jnp.float32)
    renewed = jnp.maximum(preact, jnp.float32(0.0)).astype(jnp.bfloat16)
    picked_rows = [
        lax.dot_general(
            choosers[parity], renewed, (((0,), (1,)), ((), ())), preferred_element_type=jnp.float32
        ).astype(jnp.bfloat16)
        for parity in range(2)
    ]
    back_send = jnp.concatenate(picked_rows, axis=1).reshape(n_dom, group // 2, 2 * feat_width)
    (back,) = _all_to_all([back_send], 2)
    replicas = back.reshape(n_dom, group // 2, 2, feat_width).transpose(3, 0, 1, 2)
    return (renewed, replicas.reshape(feat_width, slot_count))


def solution(mesh):
    in_specs = (
        P("feat", "dom"),
        P("dom", None, None),
        P(None, "dom"),
        P(None, "dom"),
        P("feat", "dom"),
        P(),
        P(),
    )
    out_specs = (P("feat", "dom"), P("feat", "dom"))
    body = functools.partial(per_device, mesh.shape["dom"], mesh.shape["feat"])
    return jax.shard_map(body, mesh=mesh, in_specs=in_specs, out_specs=out_specs, check_vma=False)
```

```python
import functools

import jax
import jax.numpy as jnp
from jax import lax
from jax.experimental import pallas as pl
from jax.experimental.pallas import tpu as pltpu
from jax.sharding import PartitionSpec as P

MESH = pl.DeviceIdType.MESH


def _greet(axis, n, where):
    me = lax.axis_index(axis)
    bar = pltpu.get_barrier_semaphore()

    def sig(k, carry):
        pl.semaphore_signal(bar, 1, device_id=where(lax.rem(me + k, n)), device_id_type=MESH)
        return carry

    lax.fori_loop(1, n, sig, 0, unroll=8)
    pl.semaphore_wait(bar, n - 1)
    return me


def _a2a_kernel(*refs):
    k = (len(refs) - 2) // 2
    xs, outs = refs[:k], refs[k : 2 * k]
    send_sem, recv_sem = refs[2 * k :]
    n = xs[0].shape[0]
    f = lax.axis_index("feat")
    where = lambda d: (d, f)
    me = _greet("dom", n, where)
    for i in range(k):
        pltpu.make_async_copy(xs[i].at[me], outs[i].at[me], recv_sem.at[i]).start()

    def start(j, carry):
        peer = lax.rem(me + j, n)
        for i in range(k):
            pltpu.make_async_remote_copy(
                xs[i].at[peer],
                outs[i].at[me],
                send_sem.at[i],
                recv_sem.at[i],
                device_id=where(peer),
                device_id_type=MESH,
            ).start()
        return carry

    lax.fori_loop(1, n, start, 0, unroll=8)
    for i in range(k):
        sent = xs[i].at[pl.ds(0, n - 1)]
        pltpu.make_async_copy(sent, sent, send_sem.at[i]).wait()
        pltpu.make_async_copy(outs[i], outs[i], recv_sem.at[i]).wait()


def _all_to_all(arrays, cid):
    k = len(arrays)
    return pl.pallas_call(
        _a2a_kernel,
        out_shape=[jax.ShapeDtypeStruct(a.shape, a.dtype) for a in arrays],
        in_specs=[pl.BlockSpec(memory_space=pl.ANY)] * k,
        out_specs=[pl.BlockSpec(memory_space=pl.ANY)] * k,
        scratch_shapes=[
            pltpu.SemaphoreType.DMA((k,)),
            pltpu.SemaphoreType.DMA((k,)),
        ],
        compiler_params=pltpu.CompilerParams(has_side_effects=True, collective_id=cid),
    )(*arrays)


def _gather_kernel(x_ref, o_ref, send_sem, recv_sem):
    g = o_ref.shape[0]
    d = lax.axis_index("dom")
    where = lambda q: (d, q)
    me = _greet("feat", g, where)
    right, left, far = lax.rem(me + 1, g), lax.rem(me + g - 1, g), lax.rem(me + 2, g)
    h = o_ref.shape[1] // 2

    def arrived(slot):
        pltpu.make_async_copy(o_ref.at[slot], o_ref.at[slot], recv_sem.at[slot]).wait()

    def send(src, dst, slot, peer):
        pltpu.make_async_remote_copy(
            src, dst, send_sem, recv_sem.at[slot], device_id=where(peer), device_id_type=MESH
        ).start()

    pltpu.make_async_copy(x_ref, o_ref.at[me], recv_sem.at[me]).start()
    send(x_ref, o_ref.at[me], me, right)
    send(x_ref, o_ref.at[me], me, left)
    arrived(left)
    arrived(right)
    send(o_ref.at[left, pl.ds(0, h)], o_ref.at[left, pl.ds(0, h)], left, right)
    send(o_ref.at[right, pl.ds(h, h)], o_ref.at[right, pl.ds(h, h)], right, left)
    arrived(far)
    arrived(me)
    sent = o_ref.at[pl.ds(0, g - 1)]
    pltpu.make_async_copy(sent, sent, send_sem).wait()


def _feat_gather(x, g, cid):
    return pl.pallas_call(
        _gather_kernel,
        out_shape=jax.ShapeDtypeStruct((g,) + x.shape, x.dtype),
        in_specs=[pl.BlockSpec(memory_space=pl.ANY)],
        out_specs=pl.BlockSpec(memory_space=pl.ANY),
        scratch_shapes=[pltpu.SemaphoreType.DMA(()), pltpu.SemaphoreType.DMA((g,))],
        compiler_params=pltpu.CompilerParams(has_side_effects=True, collective_id=cid),
    )(x).reshape((g * x.shape[0],) + x.shape[1:])


def per_device(n_dom, n_feat, replica_feat, adjacency_tiles, tile_index, route, node_feat, w_self, w_neigh):
    feat_width, slot_count = replica_feat.shape
    tile_side = adjacency_tiles.shape[1]
    block_count = slot_count // tile_side
    node_count = node_feat.shape[1]
    group = slot_count // n_dom
    full_feat = lax.all_gather(node_feat, "feat", axis=0, tiled=True)
    stacked = replica_feat.reshape(feat_width, block_count, tile_side)
    picked = jnp.take(stacked, tile_index[1], axis=1)
    one_hot = (tile_index[0][:, None] == jnp.arange(block_count, dtype=jnp.int32)[None, :]).astype(
        jnp.float32
    )
    product = jnp.einsum(
        "tij,ftj->tif", adjacency_tiles, picked, preferred_element_type=jnp.float32
    )
    summed = jnp.einsum("tif,tb->bif", product, one_hot, precision=lax.Precision.HIGH)
    paired = summed.astype(jnp.bfloat16)
    send = paired.reshape(n_dom, group // 2, 2 * feat_width)
    half = group // 2
    owner = lax.broadcasted_iota(jnp.int32, (n_dom, 1, group), 0)
    lane = lax.broadcasted_iota(jnp.int32, (n_dom, 1, group), 2)
    route_pairs = jnp.take(route[0], owner * group + 2 * (lane % half) + lane // half, mode="clip")
    got, got_route = _all_to_all([send, route_pairs], 0)
    got = got.reshape(slot_count // 2, 2 * feat_width)
    got_route = got_route.reshape(n_dom, 2, half)
    nodes = jnp.arange(node_count, dtype=jnp.int32)[:, None]
    choosers = [
        (got_route[:, parity, :].reshape(1, n_dom * half) == nodes).astype(jnp.bfloat16)
        for parity in range(2)
    ]
    first = (((0,), (0,)), ((), ()))
    agg = sum(
        lax.dot_general(
            got[:, parity * feat_width : (parity + 1) * feat_width],
            choosers[parity],
            (((0,), (1,)), ((), ())),
            preferred_element_type=jnp.float32,
        )
        for parity in range(2)
    ).astype(jnp.bfloat16)
    offset = lax.axis_index("feat") * feat_width
    full_agg = _feat_gather(agg, n_feat, 1)
    self_cols = lax.dynamic_slice_in_dim(w_self, offset, feat_width, 1)
    neigh_cols = lax.dynamic_slice_in_dim(w_neigh, offset, feat_width, 1)
    preact = lax.dot_general(self_cols, full_feat, first, preferred_element_type=jnp.float32)
    preact = preact + lax.dot_general(neigh_cols, full_agg, first, preferred_element_type=jnp.float32)
    renewed = jnp.maximum(preact, jnp.float32(0.0)).astype(jnp.bfloat16)
    picked_rows = [
        lax.dot_general(
            choosers[parity], renewed, (((0,), (1,)), ((), ())), preferred_element_type=jnp.float32
        ).astype(jnp.bfloat16)
        for parity in range(2)
    ]
    back_send = jnp.concatenate(picked_rows, axis=1).reshape(n_dom, group // 2, 2 * feat_width)
    (back,) = _all_to_all([back_send], 2)
    replicas = back.reshape(n_dom, group // 2, 2, feat_width).transpose(3, 0, 1, 2)
    return (renewed, replicas.reshape(feat_width, slot_count))


def solution(mesh):
    in_specs = (
        P("feat", "dom"),
        P("dom", None, None),
        P(None, "dom"),
        P(None, "dom"),
        P("feat", "dom"),
        P(),
        P(),
    )
    out_specs = (P("feat", "dom"), P("feat", "dom"))
    body = functools.partial(per_device, mesh.shape["dom"], mesh.shape["feat"])
    return jax.shard_map(body, mesh=mesh, in_specs=in_specs, out_specs=out_specs, check_vma=False)
```

```python
import functools

import jax
import jax.numpy as jnp
from jax import lax
from jax.experimental import pallas as pl
from jax.experimental.pallas import tpu as pltpu
from jax.sharding import PartitionSpec as P

MESH = pl.DeviceIdType.MESH


def _greet(axis, n, where):
    me = lax.axis_index(axis)
    bar = pltpu.get_barrier_semaphore()

    def sig(k, carry):
        pl.semaphore_signal(bar, 1, device_id=where(lax.rem(me + k, n)), device_id_type=MESH)
        return carry

    lax.fori_loop(1, n, sig, 0, unroll=True)
    pl.semaphore_wait(bar, n - 1)
    return me


def _a2a_kernel(*refs):
    k = (len(refs) - 2) // 2
    xs, outs = refs[:k], refs[k : 2 * k]
    send_sem, recv_sem = refs[2 * k :]
    n = xs[0].shape[0]
    f = lax.axis_index("feat")
    where = lambda d: (d, f)
    me = _greet("dom", n, where)
    for i in range(k):
        pltpu.make_async_copy(xs[i].at[me], outs[i].at[me], recv_sem.at[i]).start()

    def start(j, carry):
        peer = lax.rem(me + j, n)
        for i in range(k):
            pltpu.make_async_remote_copy(
                xs[i].at[peer],
                outs[i].at[me],
                send_sem.at[i],
                recv_sem.at[i],
                device_id=where(peer),
                device_id_type=MESH,
            ).start()
        return carry

    lax.fori_loop(1, n, start, 0, unroll=True)
    for i in range(k):
        sent = xs[i].at[pl.ds(0, n - 1)]
        pltpu.make_async_copy(sent, sent, send_sem.at[i]).wait()
        pltpu.make_async_copy(outs[i], outs[i], recv_sem.at[i]).wait()


def _all_to_all(arrays, cid):
    k = len(arrays)
    return pl.pallas_call(
        _a2a_kernel,
        out_shape=[jax.ShapeDtypeStruct(a.shape, a.dtype) for a in arrays],
        in_specs=[pl.BlockSpec(memory_space=pl.ANY)] * k,
        out_specs=[pl.BlockSpec(memory_space=pl.ANY)] * k,
        scratch_shapes=[
            pltpu.SemaphoreType.DMA((k,)),
            pltpu.SemaphoreType.DMA((k,)),
        ],
        compiler_params=pltpu.CompilerParams(has_side_effects=True, collective_id=cid),
    )(*arrays)


def _gather_kernel(x_ref, o_ref, send_sem, recv_sem):
    g = o_ref.shape[0]
    d = lax.axis_index("dom")
    where = lambda q: (d, q)
    me = _greet("feat", g, where)
    right, left, far = lax.rem(me + 1, g), lax.rem(me + g - 1, g), lax.rem(me + 2, g)
    h = o_ref.shape[1] // 2

    def arrived(slot):
        pltpu.make_async_copy(o_ref.at[slot], o_ref.at[slot], recv_sem.at[slot]).wait()

    def send(src, dst, slot, peer):
        pltpu.make_async_remote_copy(
            src, dst, send_sem, recv_sem.at[slot], device_id=where(peer), device_id_type=MESH
        ).start()

    pltpu.make_async_copy(x_ref, o_ref.at[me], recv_sem.at[me]).start()
    send(x_ref, o_ref.at[me], me, right)
    send(x_ref, o_ref.at[me], me, left)
    arrived(left)
    arrived(right)
    send(o_ref.at[left, pl.ds(0, h)], o_ref.at[left, pl.ds(0, h)], left, right)
    send(o_ref.at[right, pl.ds(h, h)], o_ref.at[right, pl.ds(h, h)], right, left)
    arrived(far)
    arrived(me)
    sent = o_ref.at[pl.ds(0, g - 1)]
    pltpu.make_async_copy(sent, sent, send_sem).wait()


def _feat_gather(x, g, cid):
    return pl.pallas_call(
        _gather_kernel,
        out_shape=jax.ShapeDtypeStruct((g,) + x.shape, x.dtype),
        in_specs=[pl.BlockSpec(memory_space=pl.ANY)],
        out_specs=pl.BlockSpec(memory_space=pl.ANY),
        scratch_shapes=[pltpu.SemaphoreType.DMA(()), pltpu.SemaphoreType.DMA((g,))],
        compiler_params=pltpu.CompilerParams(has_side_effects=True, collective_id=cid),
    )(x).reshape((g * x.shape[0],) + x.shape[1:])


def per_device(n_dom, n_feat, replica_feat, adjacency_tiles, tile_index, route, node_feat, w_self, w_neigh):
    feat_width, slot_count = replica_feat.shape
    tile_side = adjacency_tiles.shape[1]
    block_count = slot_count // tile_side
    node_count = node_feat.shape[1]
    group = slot_count // n_dom
    full_feat = lax.all_gather(node_feat, "feat", axis=0, tiled=True)
    stacked = replica_feat.reshape(feat_width, block_count, tile_side)
    picked = jnp.take(stacked, tile_index[1], axis=1)
    one_hot = (tile_index[0][:, None] == jnp.arange(block_count, dtype=jnp.int32)[None, :]).astype(
        jnp.float32
    )
    product = jnp.einsum(
        "tij,ftj->tif", adjacency_tiles, picked, preferred_element_type=jnp.float32
    )
    summed = jnp.einsum("tif,tb->bif", product, one_hot, precision=lax.Precision.HIGH)
    paired = summed.astype(jnp.bfloat16)
    send = paired.reshape(n_dom, group // 2, 2 * feat_width)
    half = group // 2
    route_pairs = route.reshape(n_dom, half, 2).transpose(0, 2, 1).reshape(n_dom, 1, group)
    got, got_route = _all_to_all([send, route_pairs], 0)
    got = got.reshape(slot_count // 2, 2 * feat_width)
    got_route = got_route.reshape(n_dom, 2, half)
    nodes = jnp.arange(node_count, dtype=jnp.int32)[:, None]
    choosers = [
        (got_route[:, parity, :].reshape(1, n_dom * half) == nodes).astype(jnp.bfloat16)
        for parity in range(2)
    ]
    first = (((0,), (0,)), ((), ()))
    agg = sum(
        lax.dot_general(
            got[:, parity * feat_width : (parity + 1) * feat_width],
            choosers[parity],
            (((0,), (1,)), ((), ())),
            preferred_element_type=jnp.float32,
        )
        for parity in range(2)
    ).astype(jnp.bfloat16)
    offset = lax.axis_index("feat") * feat_width
    full_agg = _feat_gather(agg, n_feat, 1)
    self_cols = lax.dynamic_slice_in_dim(w_self, offset, feat_width, 1)
    neigh_cols = lax.dynamic_slice_in_dim(w_neigh, offset, feat_width, 1)
    preact = lax.dot_general(self_cols, full_feat, first, preferred_element_type=jnp.float32)
    preact = preact + lax.dot_general(neigh_cols, full_agg, first, preferred_element_type=jnp.float32)
    renewed = jnp.maximum(preact, jnp.float32(0.0)).astype(jnp.bfloat16)
    picked_rows = [
        lax.dot_general(
            choosers[parity], renewed, (((0,), (1,)), ((), ())), preferred_element_type=jnp.float32
        ).astype(jnp.bfloat16)
        for parity in range(2)
    ]
    back_send = jnp.concatenate(picked_rows, axis=1).reshape(n_dom, group // 2, 2 * feat_width)
    (back,) = _all_to_all([back_send], 2)
    replicas = back.reshape(n_dom, group // 2, 2, feat_width).transpose(3, 0, 1, 2)
    return (renewed, replicas.reshape(feat_width, slot_count))


def solution(mesh):
    in_specs = (
        P("feat", "dom"),
        P("dom", None, None),
        P(None, "dom"),
        P(None, "dom"),
        P("feat", "dom"),
        P(),
        P(),
    )
    out_specs = (P("feat", "dom"), P("feat", "dom"))
    body = functools.partial(per_device, mesh.shape["dom"], mesh.shape["feat"])
    return jax.shard_map(body, mesh=mesh, in_specs=in_specs, out_specs=out_specs, check_vma=False)
```

```python
import functools

import jax
import jax.numpy as jnp
from jax import lax
from jax.experimental import pallas as pl
from jax.experimental.pallas import tpu as pltpu
from jax.sharding import PartitionSpec as P

MESH = pl.DeviceIdType.MESH


def _greet(axis, n, where):
    me = lax.axis_index(axis)
    bar = pltpu.get_barrier_semaphore()

    def sig(k, carry):
        pl.semaphore_signal(bar, 1, device_id=where(lax.rem(me + k, n)), device_id_type=MESH)
        return carry

    lax.fori_loop(1, n, sig, 0, unroll=8)
    pl.semaphore_wait(bar, n - 1)
    return me


def _a2a_kernel(*refs):
    k = (len(refs) - 2) // 2
    xs, outs = refs[:k], refs[k : 2 * k]
    send_sem, recv_sem = refs[2 * k :]
    n = xs[0].shape[0]
    f = lax.axis_index("feat")
    where = lambda d: (d, f)
    me = _greet("dom", n, where)
    for i in range(k):
        pltpu.make_async_copy(xs[i].at[me], outs[i].at[me], recv_sem.at[i]).start()

    def start(j, carry):
        peer = lax.rem(me + j, n)
        for i in range(k):
            pltpu.make_async_remote_copy(
                xs[i].at[peer],
                outs[i].at[me],
                send_sem.at[i],
                recv_sem.at[i],
                device_id=where(peer),
                device_id_type=MESH,
            ).start()
        return carry

    lax.fori_loop(1, n, start, 0, unroll=8)
    for i in range(k):
        sent = xs[i].at[pl.ds(0, n - 1)]
        pltpu.make_async_copy(sent, sent, send_sem.at[i]).wait()
        pltpu.make_async_copy(outs[i], outs[i], recv_sem.at[i]).wait()


def _all_to_all(arrays, cid):
    k = len(arrays)
    return pl.pallas_call(
        _a2a_kernel,
        out_shape=[jax.ShapeDtypeStruct(a.shape, a.dtype) for a in arrays],
        in_specs=[pl.BlockSpec(memory_space=pl.ANY)] * k,
        out_specs=[pl.BlockSpec(memory_space=pl.ANY)] * k,
        scratch_shapes=[
            pltpu.SemaphoreType.DMA((k,)),
            pltpu.SemaphoreType.DMA((k,)),
        ],
        compiler_params=pltpu.CompilerParams(has_side_effects=True, collective_id=cid),
    )(*arrays)


def _gather_kernel(x_ref, o_ref, send_sem, recv_sem):
    g = o_ref.shape[0]
    d = lax.axis_index("dom")
    where = lambda q: (d, q)
    me = _greet("feat", g, where)
    right, left, far = lax.rem(me + 1, g), lax.rem(me + g - 1, g), lax.rem(me + 2, g)
    h = o_ref.shape[1] // 2

    def arrived(slot):
        pltpu.make_async_copy(o_ref.at[slot], o_ref.at[slot], recv_sem.at[slot]).wait()

    def send(src, dst, slot, peer):
        pltpu.make_async_remote_copy(
            src, dst, send_sem, recv_sem.at[slot], device_id=where(peer), device_id_type=MESH
        ).start()

    pltpu.make_async_copy(x_ref, o_ref.at[me], recv_sem.at[me]).start()
    send(x_ref, o_ref.at[me], me, right)
    send(x_ref, o_ref.at[me], me, left)
    arrived(left)
    arrived(right)
    send(o_ref.at[left, pl.ds(0, h)], o_ref.at[left, pl.ds(0, h)], left, right)
    send(o_ref.at[right, pl.ds(h, h)], o_ref.at[right, pl.ds(h, h)], right, left)
    arrived(far)
    arrived(me)
    sent = o_ref.at[pl.ds(0, g - 1)]
    pltpu.make_async_copy(sent, sent, send_sem).wait()


def _feat_gather(x, g, cid):
    return pl.pallas_call(
        _gather_kernel,
        out_shape=jax.ShapeDtypeStruct((g,) + x.shape, x.dtype),
        in_specs=[pl.BlockSpec(memory_space=pl.ANY)],
        out_specs=pl.BlockSpec(memory_space=pl.ANY),
        scratch_shapes=[pltpu.SemaphoreType.DMA(()), pltpu.SemaphoreType.DMA((g,))],
        compiler_params=pltpu.CompilerParams(has_side_effects=True, collective_id=cid),
    )(x).reshape((g * x.shape[0],) + x.shape[1:])


def per_device(n_dom, n_feat, replica_feat, adjacency_tiles, tile_index, route, node_feat, w_self, w_neigh):
    feat_width, slot_count = replica_feat.shape
    tile_side = adjacency_tiles.shape[1]
    block_count = slot_count // tile_side
    node_count = node_feat.shape[1]
    group = slot_count // n_dom
    full_feat = lax.all_gather(node_feat, "feat", axis=0, tiled=True)
    stacked = replica_feat.reshape(feat_width, block_count, tile_side)
    picked = jnp.take(stacked, tile_index[1], axis=1)
    one_hot = (tile_index[0][:, None] == jnp.arange(block_count, dtype=jnp.int32)[None, :]).astype(
        jnp.float32
    )
    product = jnp.einsum(
        "tij,ftj->tif", adjacency_tiles, picked, preferred_element_type=jnp.float32
    )
    summed = jnp.einsum("tif,tb->bif", product, one_hot, precision=lax.Precision.HIGH)
    paired = summed.astype(jnp.bfloat16)
    half = group // 2
    send = paired.reshape(n_dom, 2, half, feat_width).transpose(0, 2, 1, 3)
    send = send.reshape(n_dom, half, 2 * feat_width)
    got, got_route = _all_to_all([send, route.reshape(n_dom, 1, group)], 0)
    got = got.reshape(slot_count // 2, 2 * feat_width)
    got_route = got_route.reshape(n_dom, 2, half)
    nodes = jnp.arange(node_count, dtype=jnp.int32)[:, None]
    choosers = [
        (got_route[:, parity, :].reshape(1, n_dom * half) == nodes).astype(jnp.bfloat16)
        for parity in range(2)
    ]
    first = (((0,), (0,)), ((), ()))
    agg = sum(
        lax.dot_general(
            got[:, parity * feat_width : (parity + 1) * feat_width],
            choosers[parity],
            (((0,), (1,)), ((), ())),
            preferred_element_type=jnp.float32,
        )
        for parity in range(2)
    ).astype(jnp.bfloat16)
    offset = lax.axis_index("feat") * feat_width
    full_agg = _feat_gather(agg, n_feat, 1)
    self_cols = lax.dynamic_slice_in_dim(w_self, offset, feat_width, 1)
    neigh_cols = lax.dynamic_slice_in_dim(w_neigh, offset, feat_width, 1)
    preact = lax.dot_general(self_cols, full_feat, first, preferred_element_type=jnp.float32)
    preact = preact + lax.dot_general(neigh_cols, full_agg, first, preferred_element_type=jnp.float32)
    renewed = jnp.maximum(preact, jnp.float32(0.0)).astype(jnp.bfloat16)
    picked_rows = [
        lax.dot_general(
            choosers[parity], renewed, (((0,), (1,)), ((), ())), preferred_element_type=jnp.float32
        ).astype(jnp.bfloat16)
        for parity in range(2)
    ]
    back_send = jnp.concatenate(picked_rows, axis=1).reshape(n_dom, group // 2, 2 * feat_width)
    (back,) = _all_to_all([back_send], 2)
    replicas = back.reshape(n_dom, half, 2, feat_width).transpose(3, 0, 2, 1)
    return (renewed, replicas.reshape(feat_width, slot_count))


def solution(mesh):
    in_specs = (
        P("feat", "dom"),
        P("dom", None, None),
        P(None, "dom"),
        P(None, "dom"),
        P("feat", "dom"),
        P(),
        P(),
    )
    out_specs = (P("feat", "dom"), P("feat", "dom"))
    body = functools.partial(per_device, mesh.shape["dom"], mesh.shape["feat"])
    return jax.shard_map(body, mesh=mesh, in_specs=in_specs, out_specs=out_specs, check_vma=False)
```

```python
import functools

import jax
import jax.numpy as jnp
from jax import lax
from jax.experimental import pallas as pl
from jax.experimental.pallas import tpu as pltpu
from jax.sharding import PartitionSpec as P

MESH = pl.DeviceIdType.MESH


def _greet(axis, n, where):
    me = lax.axis_index(axis)
    bar = pltpu.get_barrier_semaphore()

    def sig(k, carry):
        pl.semaphore_signal(bar, 1, device_id=where(lax.rem(me + k, n)), device_id_type=MESH)
        return carry

    lax.fori_loop(1, n, sig, 0, unroll=8)
    pl.semaphore_wait(bar, n - 1)
    return me


def _a2a_kernel(*refs):
    k = (len(refs) - 2) // 2
    xs, outs = refs[:k], refs[k : 2 * k]
    send_sem, recv_sem = refs[2 * k :]
    n = xs[0].shape[0]
    f = lax.axis_index("feat")
    where = lambda d: (d, f)
    me = _greet("dom", n, where)
    for i in range(k):
        pltpu.make_async_copy(xs[i].at[me], outs[i].at[me], recv_sem.at[i]).start()

    def start(j, carry):
        peer = lax.rem(me + j, n)
        for i in range(k):
            pltpu.make_async_remote_copy(
                xs[i].at[peer],
                outs[i].at[me],
                send_sem.at[i],
                recv_sem.at[i],
                device_id=where(peer),
                device_id_type=MESH,
            ).start()
        return carry

    lax.fori_loop(1, n, start, 0, unroll=8)
    for i in range(k):
        sent = xs[i].at[pl.ds(0, n - 1)]
        pltpu.make_async_copy(sent, sent, send_sem.at[i]).wait()
        pltpu.make_async_copy(outs[i], outs[i], recv_sem.at[i]).wait()


def _all_to_all(arrays, cid):
    k = len(arrays)
    return pl.pallas_call(
        _a2a_kernel,
        out_shape=[jax.ShapeDtypeStruct(a.shape, a.dtype) for a in arrays],
        in_specs=[pl.BlockSpec(memory_space=pl.ANY)] * k,
        out_specs=[pl.BlockSpec(memory_space=pl.ANY)] * k,
        scratch_shapes=[
            pltpu.SemaphoreType.DMA((k,)),
            pltpu.SemaphoreType.DMA((k,)),
        ],
        compiler_params=pltpu.CompilerParams(has_side_effects=True, collective_id=cid),
    )(*arrays)


def _gather_kernel(x_ref, o_ref, send_sem, recv_sem):
    g = o_ref.shape[0]
    d = lax.axis_index("dom")
    where = lambda q: (d, q)
    me = _greet("feat", g, where)
    right, left, far = lax.rem(me + 1, g), lax.rem(me + g - 1, g), lax.rem(me + 2, g)
    h = o_ref.shape[1] // 2

    def arrived(slot):
        pltpu.make_async_copy(o_ref.at[slot], o_ref.at[slot], recv_sem.at[slot]).wait()

    def send(src, dst, slot, peer):
        pltpu.make_async_remote_copy(
            src, dst, send_sem, recv_sem.at[slot], device_id=where(peer), device_id_type=MESH
        ).start()

    pltpu.make_async_copy(x_ref, o_ref.at[me], recv_sem.at[me]).start()
    send(x_ref, o_ref.at[me], me, right)
    send(x_ref, o_ref.at[me], me, left)
    arrived(left)
    arrived(right)
    send(o_ref.at[left, pl.ds(0, h)], o_ref.at[left, pl.ds(0, h)], left, right)
    send(o_ref.at[right, pl.ds(h, h)], o_ref.at[right, pl.ds(h, h)], right, left)
    arrived(far)
    arrived(me)
    sent = o_ref.at[pl.ds(0, g - 1)]
    pltpu.make_async_copy(sent, sent, send_sem).wait()


def _feat_gather(x, g, cid):
    return pl.pallas_call(
        _gather_kernel,
        out_shape=jax.ShapeDtypeStruct((g,) + x.shape, x.dtype),
        in_specs=[pl.BlockSpec(memory_space=pl.ANY)],
        out_specs=pl.BlockSpec(memory_space=pl.ANY),
        scratch_shapes=[pltpu.SemaphoreType.DMA(()), pltpu.SemaphoreType.DMA((g,))],
        compiler_params=pltpu.CompilerParams(has_side_effects=True, collective_id=cid),
    )(x).reshape((g * x.shape[0],) + x.shape[1:])


def per_device(n_dom, n_feat, replica_feat, adjacency_tiles, tile_index, route, node_feat, w_self, w_neigh):
    feat_width, slot_count = replica_feat.shape
    tile_side = adjacency_tiles.shape[1]
    block_count = slot_count // tile_side
    node_count = node_feat.shape[1]
    group = slot_count // n_dom
    full_feat = lax.all_gather(node_feat, "feat", axis=0, tiled=True)
    stacked = replica_feat.reshape(feat_width, block_count, tile_side)
    picked = jnp.take(stacked, tile_index[1], axis=1)
    one_hot = (tile_index[0][:, None] == jnp.arange(block_count, dtype=jnp.int32)[None, :]).astype(
        jnp.float32
    )
    product = jnp.einsum(
        "tij,ftj->tif", adjacency_tiles, picked, preferred_element_type=jnp.float32
    )
    summed = jnp.einsum("tif,tb->bif", product, one_hot, precision=lax.Precision.HIGH)
    paired = summed.astype(jnp.bfloat16)
    half = group // 2
    send = paired.reshape(n_dom, 2, half, feat_width).transpose(0, 2, 1, 3)
    send = send.reshape(n_dom, half, 2 * feat_width)
    got, got_route = _all_to_all([send, route.reshape(n_dom, 1, group)], 0)
    got = got.reshape(slot_count // 2, 2 * feat_width)
    got_route = got_route.reshape(n_dom, 2, half)
    nodes = jnp.arange(node_count, dtype=jnp.int32)[:, None]
    choosers = [
        (got_route[:, parity, :].reshape(1, n_dom * half) == nodes).astype(jnp.bfloat16)
        for parity in range(2)
    ]
    first = (((0,), (0,)), ((), ()))
    agg = sum(
        lax.dot_general(
            got[:, parity * feat_width : (parity + 1) * feat_width],
            choosers[parity],
            (((0,), (1,)), ((), ())),
            preferred_element_type=jnp.float32,
        )
        for parity in range(2)
    ).astype(jnp.bfloat16)
    offset = lax.axis_index("feat") * feat_width
    full_agg = _feat_gather(agg, n_feat, 1)
    self_cols = lax.dynamic_slice_in_dim(w_self, offset, feat_width, 1)
    neigh_cols = lax.dynamic_slice_in_dim(w_neigh, offset, feat_width, 1)
    preact = lax.dot_general(self_cols, full_feat, first, preferred_element_type=jnp.float32)
    preact = preact + lax.dot_general(neigh_cols, full_agg, first, preferred_element_type=jnp.float32)
    renewed = jnp.maximum(preact, jnp.float32(0.0)).astype(jnp.bfloat16)
    picked_rows = [
        lax.dot_general(
            choosers[parity], renewed, (((0,), (1,)), ((), ())), preferred_element_type=jnp.float32
        ).astype(jnp.bfloat16)
        for parity in range(2)
    ]
    back_send = jnp.concatenate(picked_rows, axis=1).reshape(n_dom, group // 2, 2 * feat_width)
    (back,) = _all_to_all([back_send], 2)
    flipped = back.reshape(n_dom * half, 2 * feat_width).T
    replicas = flipped.reshape(2, feat_width, n_dom, half).transpose(1, 2, 0, 3)
    return (renewed, replicas.reshape(feat_width, slot_count))


def solution(mesh):
    in_specs = (
        P("feat", "dom"),
        P("dom", None, None),
        P(None, "dom"),
        P(None, "dom"),
        P("feat", "dom"),
        P(),
        P(),
    )
    out_specs = (P("feat", "dom"), P("feat", "dom"))
    body = functools.partial(per_device, mesh.shape["dom"], mesh.shape["feat"])
    return jax.shard_map(body, mesh=mesh, in_specs=in_specs, out_specs=out_specs, check_vma=False)
```

```python
import functools

import jax
import jax.numpy as jnp
from jax import lax
from jax.experimental import pallas as pl
from jax.experimental.pallas import tpu as pltpu
from jax.sharding import PartitionSpec as P

MESH = pl.DeviceIdType.MESH


def _greet(axis, n, where):
    me = lax.axis_index(axis)
    bar = pltpu.get_barrier_semaphore()

    def sig(k, carry):
        pl.semaphore_signal(bar, 1, device_id=where(lax.rem(me + k, n)), device_id_type=MESH)
        return carry

    lax.fori_loop(1, n, sig, 0, unroll=8)
    pl.semaphore_wait(bar, n - 1)
    return me


def _a2a_kernel(*refs):
    k = (len(refs) - 2) // 2
    xs, outs = refs[:k], refs[k : 2 * k]
    send_sem, recv_sem = refs[2 * k :]
    n = xs[0].shape[0]
    f = lax.axis_index("feat")
    where = lambda d: (d, f)
    me = _greet("dom", n, where)
    for i in range(k):
        pltpu.make_async_copy(xs[i].at[me], outs[i].at[me], recv_sem.at[i]).start()

    def start(j, carry):
        peer = lax.rem(me + j, n)
        for i in range(k):
            pltpu.make_async_remote_copy(
                xs[i].at[peer],
                outs[i].at[me],
                send_sem.at[i],
                recv_sem.at[i],
                device_id=where(peer),
                device_id_type=MESH,
            ).start()
        return carry

    lax.fori_loop(1, n, start, 0, unroll=8)
    for i in range(k):
        sent = xs[i].at[pl.ds(0, n - 1)]
        pltpu.make_async_copy(sent, sent, send_sem.at[i]).wait()
        pltpu.make_async_copy(outs[i], outs[i], recv_sem.at[i]).wait()


def _all_to_all(arrays, cid):
    k = len(arrays)
    return pl.pallas_call(
        _a2a_kernel,
        out_shape=[jax.ShapeDtypeStruct(a.shape, a.dtype) for a in arrays],
        in_specs=[pl.BlockSpec(memory_space=pl.ANY)] * k,
        out_specs=[pl.BlockSpec(memory_space=pl.ANY)] * k,
        scratch_shapes=[
            pltpu.SemaphoreType.DMA((k,)),
            pltpu.SemaphoreType.DMA((k,)),
        ],
        compiler_params=pltpu.CompilerParams(has_side_effects=True, collective_id=cid),
    )(*arrays)


def _gather_kernel(x_ref, o_ref, send_sem, recv_sem):
    g = o_ref.shape[0]
    d = lax.axis_index("dom")
    where = lambda q: (d, q)
    me = _greet("feat", g, where)
    right, left, far = lax.rem(me + 1, g), lax.rem(me + g - 1, g), lax.rem(me + 2, g)
    h = o_ref.shape[1] // 2

    def arrived(slot):
        pltpu.make_async_copy(o_ref.at[slot], o_ref.at[slot], recv_sem.at[slot]).wait()

    def send(src, dst, slot, peer):
        pltpu.make_async_remote_copy(
            src, dst, send_sem, recv_sem.at[slot], device_id=where(peer), device_id_type=MESH
        ).start()

    pltpu.make_async_copy(x_ref, o_ref.at[me], recv_sem.at[me]).start()
    send(x_ref, o_ref.at[me], me, right)
    send(x_ref, o_ref.at[me], me, left)
    arrived(left)
    arrived(right)
    send(o_ref.at[left, pl.ds(0, h)], o_ref.at[left, pl.ds(0, h)], left, right)
    send(o_ref.at[right, pl.ds(h, h)], o_ref.at[right, pl.ds(h, h)], right, left)
    arrived(far)
    arrived(me)
    sent = o_ref.at[pl.ds(0, g - 1)]
    pltpu.make_async_copy(sent, sent, send_sem).wait()


def _feat_gather(x, g, cid):
    return pl.pallas_call(
        _gather_kernel,
        out_shape=jax.ShapeDtypeStruct((g,) + x.shape, x.dtype),
        in_specs=[pl.BlockSpec(memory_space=pl.ANY)],
        out_specs=pl.BlockSpec(memory_space=pl.ANY),
        scratch_shapes=[pltpu.SemaphoreType.DMA(()), pltpu.SemaphoreType.DMA((g,))],
        compiler_params=pltpu.CompilerParams(has_side_effects=True, collective_id=cid),
    )(x).reshape((g * x.shape[0],) + x.shape[1:])


def per_device(n_dom, n_feat, replica_feat, adjacency_tiles, tile_index, route, node_feat, w_self, w_neigh):
    feat_width, slot_count = replica_feat.shape
    tile_side = adjacency_tiles.shape[1]
    block_count = slot_count // tile_side
    node_count = node_feat.shape[1]
    group = slot_count // n_dom
    full_feat = lax.all_gather(node_feat, "feat", axis=0, tiled=True)
    stacked = replica_feat.reshape(feat_width, block_count, tile_side)
    picked = jnp.take(stacked, tile_index[1], axis=1)
    one_hot = (tile_index[0][:, None] == jnp.arange(block_count, dtype=jnp.int32)[None, :]).astype(
        jnp.float32
    )
    product = jnp.einsum(
        "tij,ftj->tif", adjacency_tiles, picked, preferred_element_type=jnp.float32
    )
    summed = jnp.einsum("tif,tb->bif", product, one_hot, precision=lax.Precision.HIGH)
    paired = summed.astype(jnp.bfloat16)
    half = group // 2
    send = paired.reshape(n_dom, 2, half, feat_width).transpose(0, 2, 1, 3)
    send = send.reshape(n_dom, half, 2 * feat_width)
    got, got_route = _all_to_all([send, route.reshape(n_dom, 1, group)], 0)
    got = got.reshape(slot_count // 2, 2 * feat_width)
    got_route = got_route.reshape(n_dom, 2, half)
    nodes = jnp.arange(node_count, dtype=jnp.int32)[:, None]
    choosers = [
        (got_route[:, parity, :].reshape(1, n_dom * half) == nodes).astype(jnp.bfloat16)
        for parity in range(2)
    ]
    first = (((0,), (0,)), ((), ()))
    agg_t = sum(
        jnp.dot(
            choosers[parity],
            got[:, parity * feat_width : (parity + 1) * feat_width],
            preferred_element_type=jnp.float32,
        )
        for parity in range(2)
    ).astype(jnp.bfloat16)
    offset = lax.axis_index("feat") * feat_width
    full_agg_t = _feat_gather(agg_t, n_feat, 1).reshape(n_feat, node_count, feat_width)
    self_cols = lax.dynamic_slice_in_dim(w_self, offset, feat_width, 1)
    neigh_cols = lax.dynamic_slice_in_dim(w_neigh, offset, feat_width, 1)
    preact = lax.dot_general(self_cols, full_feat, first, preferred_element_type=jnp.float32)
    neigh_cols = neigh_cols.reshape(n_feat, feat_width, feat_width)
    preact = preact + lax.dot_general(
        neigh_cols, full_agg_t, (((0, 1), (0, 2)), ((), ())), preferred_element_type=jnp.float32
    )
    renewed = jnp.maximum(preact, jnp.float32(0.0)).astype(jnp.bfloat16)
    picked_rows = [
        lax.dot_general(
            choosers[parity], renewed, (((0,), (1,)), ((), ())), preferred_element_type=jnp.float32
        ).astype(jnp.bfloat16)
        for parity in range(2)
    ]
    back_send = jnp.concatenate(picked_rows, axis=1).reshape(n_dom, group // 2, 2 * feat_width)
    (back,) = _all_to_all([back_send], 2)
    replicas = back.reshape(n_dom, half, 2, feat_width).transpose(3, 0, 2, 1)
    return (renewed, replicas.reshape(feat_width, slot_count))


def solution(mesh):
    in_specs = (
        P("feat", "dom"),
        P("dom", None, None),
        P(None, "dom"),
        P(None, "dom"),
        P("feat", "dom"),
        P(),
        P(),
    )
    out_specs = (P("feat", "dom"), P("feat", "dom"))
    body = functools.partial(per_device, mesh.shape["dom"], mesh.shape["feat"])
    return jax.shard_map(body, mesh=mesh, in_specs=in_specs, out_specs=out_specs, check_vma=False)
```

```python
import functools

import jax
import jax.numpy as jnp
from jax import lax
from jax.experimental import pallas as pl
from jax.experimental.pallas import tpu as pltpu
from jax.sharding import PartitionSpec as P

MESH = pl.DeviceIdType.MESH


def _greet(axis, n, where):
    me = lax.axis_index(axis)
    bar = pltpu.get_barrier_semaphore()

    def sig(k, carry):
        pl.semaphore_signal(bar, 1, device_id=where(lax.rem(me + k, n)), device_id_type=MESH)
        return carry

    lax.fori_loop(1, n, sig, 0, unroll=8)
    pl.semaphore_wait(bar, n - 1)
    return me


def _a2a_kernel(*refs):
    k = (len(refs) - 2) // 2
    xs, outs = refs[:k], refs[k : 2 * k]
    send_sem, recv_sem = refs[2 * k :]
    n = xs[0].shape[0]
    f = lax.axis_index("feat")
    where = lambda d: (d, f)
    me = _greet("dom", n, where)
    for i in range(k):
        pltpu.make_async_copy(xs[i].at[me], outs[i].at[me], recv_sem.at[i]).start()

    def start(j, carry):
        peer = lax.rem(me + j, n)
        for i in range(k):
            pltpu.make_async_remote_copy(
                xs[i].at[peer],
                outs[i].at[me],
                send_sem.at[i],
                recv_sem.at[i],
                device_id=where(peer),
                device_id_type=MESH,
            ).start()
        return carry

    lax.fori_loop(1, n, start, 0, unroll=8)
    for i in range(k):
        sent = xs[i].at[pl.ds(0, n - 1)]
        pltpu.make_async_copy(sent, sent, send_sem.at[i]).wait()
        pltpu.make_async_copy(outs[i], outs[i], recv_sem.at[i]).wait()


def _all_to_all(arrays, cid):
    k = len(arrays)
    return pl.pallas_call(
        _a2a_kernel,
        out_shape=[jax.ShapeDtypeStruct(a.shape, a.dtype) for a in arrays],
        in_specs=[pl.BlockSpec(memory_space=pl.ANY)] * k,
        out_specs=[pl.BlockSpec(memory_space=pl.ANY)] * k,
        scratch_shapes=[
            pltpu.SemaphoreType.DMA((k,)),
            pltpu.SemaphoreType.DMA((k,)),
        ],
        compiler_params=pltpu.CompilerParams(has_side_effects=True, collective_id=cid),
    )(*arrays)


def _gather_kernel(x_ref, o_ref, send_sem, recv_sem):
    g = o_ref.shape[0]
    d = lax.axis_index("dom")
    where = lambda q: (d, q)
    me = _greet("feat", g, where)
    right, left, far = lax.rem(me + 1, g), lax.rem(me + g - 1, g), lax.rem(me + 2, g)
    h = o_ref.shape[1] // 2

    def arrived(slot):
        pltpu.make_async_copy(o_ref.at[slot], o_ref.at[slot], recv_sem.at[slot]).wait()

    def send(src, dst, slot, peer):
        pltpu.make_async_remote_copy(
            src, dst, send_sem, recv_sem.at[slot], device_id=where(peer), device_id_type=MESH
        ).start()

    pltpu.make_async_copy(x_ref, o_ref.at[me], recv_sem.at[me]).start()
    send(x_ref, o_ref.at[me], me, right)
    send(x_ref, o_ref.at[me], me, left)
    arrived(left)
    arrived(right)
    send(o_ref.at[left, pl.ds(0, h)], o_ref.at[left, pl.ds(0, h)], left, right)
    send(o_ref.at[right, pl.ds(h, h)], o_ref.at[right, pl.ds(h, h)], right, left)
    arrived(far)
    arrived(me)
    sent = o_ref.at[pl.ds(0, g - 1)]
    pltpu.make_async_copy(sent, sent, send_sem).wait()


def _feat_gather(x, g, cid):
    return pl.pallas_call(
        _gather_kernel,
        out_shape=jax.ShapeDtypeStruct((g,) + x.shape, x.dtype),
        in_specs=[pl.BlockSpec(memory_space=pltpu.VMEM)],
        out_specs=pl.BlockSpec(memory_space=pl.ANY),
        scratch_shapes=[pltpu.SemaphoreType.DMA(()), pltpu.SemaphoreType.DMA((g,))],
        compiler_params=pltpu.CompilerParams(has_side_effects=True, collective_id=cid),
    )(x).reshape((g * x.shape[0],) + x.shape[1:])


def per_device(n_dom, n_feat, replica_feat, adjacency_tiles, tile_index, route, node_feat, w_self, w_neigh):
    feat_width, slot_count = replica_feat.shape
    tile_side = adjacency_tiles.shape[1]
    block_count = slot_count // tile_side
    node_count = node_feat.shape[1]
    group = slot_count // n_dom
    full_feat = lax.all_gather(node_feat, "feat", axis=0, tiled=True)
    stacked = replica_feat.reshape(feat_width, block_count, tile_side)
    picked = jnp.take(stacked, tile_index[1], axis=1)
    one_hot = (tile_index[0][:, None] == jnp.arange(block_count, dtype=jnp.int32)[None, :]).astype(
        jnp.float32
    )
    product = jnp.einsum(
        "tij,ftj->tif", adjacency_tiles, picked, preferred_element_type=jnp.float32
    )
    summed = jnp.einsum("tif,tb->bif", product, one_hot, precision=lax.Precision.HIGH)
    paired = summed.astype(jnp.bfloat16)
    half = group // 2
    send = paired.reshape(n_dom, 2, half, feat_width).transpose(0, 2, 1, 3)
    send = send.reshape(n_dom, half, 2 * feat_width)
    got, got_route = _all_to_all([send, route.reshape(n_dom, 1, group)], 0)
    got = got.reshape(slot_count // 2, 2 * feat_width)
    got_route = got_route.reshape(n_dom, 2, half)
    nodes = jnp.arange(node_count, dtype=jnp.int32)[:, None]
    choosers = [
        (got_route[:, parity, :].reshape(1, n_dom * half) == nodes).astype(jnp.bfloat16)
        for parity in range(2)
    ]
    first = (((0,), (0,)), ((), ()))
    agg = sum(
        lax.dot_general(
            got[:, parity * feat_width : (parity + 1) * feat_width],
            choosers[parity],
            (((0,), (1,)), ((), ())),
            preferred_element_type=jnp.float32,
        )
        for parity in range(2)
    ).astype(jnp.bfloat16)
    offset = lax.axis_index("feat") * feat_width
    full_agg = _feat_gather(agg, n_feat, 1)
    self_cols = lax.dynamic_slice_in_dim(w_self, offset, feat_width, 1)
    neigh_cols = lax.dynamic_slice_in_dim(w_neigh, offset, feat_width, 1)
    preact = lax.dot_general(self_cols, full_feat, first, preferred_element_type=jnp.float32)
    preact = preact + lax.dot_general(neigh_cols, full_agg, first, preferred_element_type=jnp.float32)
    renewed = jnp.maximum(preact, jnp.float32(0.0)).astype(jnp.bfloat16)
    picked_rows = [
        lax.dot_general(
            choosers[parity], renewed, (((0,), (1,)), ((), ())), preferred_element_type=jnp.float32
        ).astype(jnp.bfloat16)
        for parity in range(2)
    ]
    back_send = jnp.concatenate(picked_rows, axis=1).reshape(n_dom, group // 2, 2 * feat_width)
    (back,) = _all_to_all([back_send], 2)
    replicas = back.reshape(n_dom, half, 2, feat_width).transpose(3, 0, 2, 1)
    return (renewed, replicas.reshape(feat_width, slot_count))


def solution(mesh):
    in_specs = (
        P("feat", "dom"),
        P("dom", None, None),
        P(None, "dom"),
        P(None, "dom"),
        P("feat", "dom"),
        P(),
        P(),
    )
    out_specs = (P("feat", "dom"), P("feat", "dom"))
    body = functools.partial(per_device, mesh.shape["dom"], mesh.shape["feat"])
    return jax.shard_map(body, mesh=mesh, in_specs=in_specs, out_specs=out_specs, check_vma=False)
```

```python
import functools

import jax
import jax.numpy as jnp
from jax import lax
from jax.experimental import pallas as pl
from jax.experimental.pallas import tpu as pltpu
from jax.sharding import PartitionSpec as P

MESH = pl.DeviceIdType.MESH


def _greet(axis, n, where):
    me = lax.axis_index(axis)
    bar = pltpu.get_barrier_semaphore()

    def sig(k, carry):
        pl.semaphore_signal(bar, 1, device_id=where(lax.rem(me + k, n)), device_id_type=MESH)
        return carry

    lax.fori_loop(1, n, sig, 0, unroll=8)
    pl.semaphore_wait(bar, n - 1)
    return me


def _a2a_kernel(*refs):
    k = (len(refs) - 2) // 2
    xs, outs = refs[:k], refs[k : 2 * k]
    send_sem, recv_sem = refs[2 * k :]
    n = xs[0].shape[0]
    f = lax.axis_index("feat")
    where = lambda d: (d, f)
    me = _greet("dom", n, where)
    for i in range(k):
        pltpu.make_async_copy(xs[i].at[me], outs[i].at[me], recv_sem.at[i]).start()

    def start(j, carry):
        peer = lax.rem(me + j, n)
        for i in range(k):
            pltpu.make_async_remote_copy(
                xs[i].at[peer],
                outs[i].at[me],
                send_sem.at[i],
                recv_sem.at[i],
                device_id=where(peer),
                device_id_type=MESH,
            ).start()
        return carry

    lax.fori_loop(1, n, start, 0, unroll=8)
    for i in range(k):
        sent = xs[i].at[pl.ds(0, n - 1)]
        pltpu.make_async_copy(sent, sent, send_sem.at[i]).wait()
        pltpu.make_async_copy(outs[i], outs[i], recv_sem.at[i]).wait()


def _all_to_all(arrays, cid):
    k = len(arrays)
    return pl.pallas_call(
        _a2a_kernel,
        out_shape=[jax.ShapeDtypeStruct(a.shape, a.dtype) for a in arrays],
        in_specs=[pl.BlockSpec(memory_space=pl.ANY)] * k,
        out_specs=[pl.BlockSpec(memory_space=pl.ANY)] * k,
        scratch_shapes=[
            pltpu.SemaphoreType.DMA((k,)),
            pltpu.SemaphoreType.DMA((k,)),
        ],
        compiler_params=pltpu.CompilerParams(has_side_effects=True, collective_id=cid),
    )(*arrays)


def _gather_kernel(x_ref, o_ref, send_sem, recv_sem):
    g = o_ref.shape[0]
    d = lax.axis_index("dom")
    where = lambda q: (d, q)
    me = _greet("feat", g, where)
    right, left, far = lax.rem(me + 1, g), lax.rem(me + g - 1, g), lax.rem(me + 2, g)
    h = o_ref.shape[1] // 2

    def arrived(slot):
        pltpu.make_async_copy(o_ref.at[slot], o_ref.at[slot], recv_sem.at[slot]).wait()

    def send(src, dst, slot, peer):
        pltpu.make_async_remote_copy(
            src, dst, send_sem, recv_sem.at[slot], device_id=where(peer), device_id_type=MESH
        ).start()

    pltpu.make_async_copy(x_ref, o_ref.at[me], recv_sem.at[me]).start()
    send(x_ref, o_ref.at[me], me, right)
    send(x_ref, o_ref.at[me], me, left)
    arrived(left)
    arrived(right)
    send(o_ref.at[left, pl.ds(0, h)], o_ref.at[left, pl.ds(0, h)], left, right)
    send(o_ref.at[right, pl.ds(h, h)], o_ref.at[right, pl.ds(h, h)], right, left)
    arrived(far)
    arrived(me)
    sent = o_ref.at[pl.ds(0, g - 1)]
    pltpu.make_async_copy(sent, sent, send_sem).wait()


def _feat_gather(x, g, cid):
    return pl.pallas_call(
        _gather_kernel,
        out_shape=jax.ShapeDtypeStruct((g,) + x.shape, x.dtype),
        in_specs=[pl.BlockSpec(memory_space=pl.ANY)],
        out_specs=pl.BlockSpec(memory_space=pl.ANY),
        scratch_shapes=[pltpu.SemaphoreType.DMA(()), pltpu.SemaphoreType.DMA((g,))],
        compiler_params=pltpu.CompilerParams(has_side_effects=True, collective_id=cid),
    )(x).reshape((g * x.shape[0],) + x.shape[1:])


def per_device(n_dom, n_feat, replica_feat, adjacency_tiles, tile_index, route, node_feat, w_self, w_neigh):
    feat_width, slot_count = replica_feat.shape
    tile_side = adjacency_tiles.shape[1]
    block_count = slot_count // tile_side
    node_count = node_feat.shape[1]
    group = slot_count // n_dom
    full_feat = lax.all_gather(node_feat, "feat", axis=0, tiled=True)
    stacked = replica_feat.reshape(feat_width, block_count, tile_side)
    source = (tile_index[1][:, None] == jnp.arange(block_count, dtype=jnp.int32)[None, :]).astype(
        jnp.bfloat16
    )
    picked = jnp.einsum(
        "fsj,ts->ftj", stacked, source, preferred_element_type=jnp.float32
    ).astype(jnp.bfloat16)
    one_hot = (tile_index[0][:, None] == jnp.arange(block_count, dtype=jnp.int32)[None, :]).astype(
        jnp.float32
    )
    product = jnp.einsum(
        "tij,ftj->tif", adjacency_tiles, picked, preferred_element_type=jnp.float32
    )
    summed = jnp.einsum("tif,tb->bif", product, one_hot, precision=lax.Precision.HIGH)
    paired = summed.astype(jnp.bfloat16)
    half = group // 2
    send = paired.reshape(n_dom, 2, half, feat_width).transpose(0, 2, 1, 3)
    send = send.reshape(n_dom, half, 2 * feat_width)
    got, got_route = _all_to_all([send, route.reshape(n_dom, 1, group)], 0)
    got = got.reshape(slot_count // 2, 2 * feat_width)
    got_route = got_route.reshape(n_dom, 2, half)
    nodes = jnp.arange(node_count, dtype=jnp.int32)[:, None]
    choosers = [
        (got_route[:, parity, :].reshape(1, n_dom * half) == nodes).astype(jnp.bfloat16)
        for parity in range(2)
    ]
    first = (((0,), (0,)), ((), ()))
    agg = sum(
        lax.dot_general(
            got[:, parity * feat_width : (parity + 1) * feat_width],
            choosers[parity],
            (((0,), (1,)), ((), ())),
            preferred_element_type=jnp.float32,
        )
        for parity in range(2)
    ).astype(jnp.bfloat16)
    offset = lax.axis_index("feat") * feat_width
    full_agg = _feat_gather(agg, n_feat, 1)
    self_cols = lax.dynamic_slice_in_dim(w_self, offset, feat_width, 1)
    neigh_cols = lax.dynamic_slice_in_dim(w_neigh, offset, feat_width, 1)
    preact = lax.dot_general(self_cols, full_feat, first, preferred_element_type=jnp.float32)
    preact = preact + lax.dot_general(neigh_cols, full_agg, first, preferred_element_type=jnp.float32)
    renewed = jnp.maximum(preact, jnp.float32(0.0)).astype(jnp.bfloat16)
    picked_rows = [
        lax.dot_general(
            choosers[parity], renewed, (((0,), (1,)), ((), ())), preferred_element_type=jnp.float32
        ).astype(jnp.bfloat16)
        for parity in range(2)
    ]
    back_send = jnp.concatenate(picked_rows, axis=1).reshape(n_dom, group // 2, 2 * feat_width)
    (back,) = _all_to_all([back_send], 2)
    replicas = back.reshape(n_dom, half, 2, feat_width).transpose(3, 0, 2, 1)
    return (renewed, replicas.reshape(feat_width, slot_count))


def solution(mesh):
    in_specs = (
        P("feat", "dom"),
        P("dom", None, None),
        P(None, "dom"),
        P(None, "dom"),
        P("feat", "dom"),
        P(),
        P(),
    )
    out_specs = (P("feat", "dom"), P("feat", "dom"))
    body = functools.partial(per_device, mesh.shape["dom"], mesh.shape["feat"])
    return jax.shard_map(body, mesh=mesh, in_specs=in_specs, out_specs=out_specs, check_vma=False)
```

```python
import functools

import jax
import jax.numpy as jnp
from jax import lax
from jax.experimental import pallas as pl
from jax.experimental.pallas import tpu as pltpu
from jax.sharding import PartitionSpec as P

MESH = pl.DeviceIdType.MESH


def _greet(axis, n, where):
    me = lax.axis_index(axis)
    bar = pltpu.get_barrier_semaphore()

    def sig(k, carry):
        pl.semaphore_signal(bar, 1, device_id=where(lax.rem(me + k, n)), device_id_type=MESH)
        return carry

    lax.fori_loop(1, n, sig, 0, unroll=8)
    pl.semaphore_wait(bar, n - 1)
    return me


def _a2a_kernel(*refs):
    k = (len(refs) - 2) // 2
    xs, outs = refs[:k], refs[k : 2 * k]
    send_sem, recv_sem = refs[2 * k :]
    n = xs[0].shape[0]
    f = lax.axis_index("feat")
    where = lambda d: (d, f)
    me = _greet("dom", n, where)
    for i in range(k):
        pltpu.make_async_copy(xs[i].at[me], outs[i].at[me], recv_sem.at[i]).start()

    def start(j, carry):
        peer = lax.rem(me + j, n)
        for i in range(k):
            pltpu.make_async_remote_copy(
                xs[i].at[peer],
                outs[i].at[me],
                send_sem.at[i],
                recv_sem.at[i],
                device_id=where(peer),
                device_id_type=MESH,
            ).start()
        return carry

    lax.fori_loop(1, n, start, 0, unroll=8)
    for i in range(k):
        sent = xs[i].at[pl.ds(0, n - 1)]
        pltpu.make_async_copy(sent, sent, send_sem.at[i]).wait()
        pltpu.make_async_copy(outs[i], outs[i], recv_sem.at[i]).wait()


def _all_to_all(arrays, cid):
    k = len(arrays)
    return pl.pallas_call(
        _a2a_kernel,
        out_shape=[jax.ShapeDtypeStruct(a.shape, a.dtype) for a in arrays],
        in_specs=[pl.BlockSpec(memory_space=pl.ANY)] * k,
        out_specs=[pl.BlockSpec(memory_space=pl.ANY)] * k,
        scratch_shapes=[
            pltpu.SemaphoreType.DMA((k,)),
            pltpu.SemaphoreType.DMA((k,)),
        ],
        compiler_params=pltpu.CompilerParams(has_side_effects=True, collective_id=cid),
    )(*arrays)


def _gather_kernel(x_ref, o_ref, send_sem, recv_sem):
    g = o_ref.shape[0]
    d = lax.axis_index("dom")
    where = lambda q: (d, q)
    me = _greet("feat", g, where)
    right, left, far = lax.rem(me + 1, g), lax.rem(me + g - 1, g), lax.rem(me + 2, g)
    h = o_ref.shape[1] // 2

    def arrived(slot):
        pltpu.make_async_copy(o_ref.at[slot], o_ref.at[slot], recv_sem.at[slot]).wait()

    def send(src, dst, slot, peer):
        pltpu.make_async_remote_copy(
            src, dst, send_sem, recv_sem.at[slot], device_id=where(peer), device_id_type=MESH
        ).start()

    pltpu.make_async_copy(x_ref, o_ref.at[me], recv_sem.at[me]).start()
    send(x_ref, o_ref.at[me], me, right)
    send(x_ref, o_ref.at[me], me, left)
    arrived(left)
    arrived(right)
    send(o_ref.at[left, pl.ds(0, h)], o_ref.at[left, pl.ds(0, h)], left, right)
    send(o_ref.at[right, pl.ds(h, h)], o_ref.at[right, pl.ds(h, h)], right, left)
    arrived(far)
    arrived(me)
    sent = o_ref.at[pl.ds(0, g - 1)]
    pltpu.make_async_copy(sent, sent, send_sem).wait()


def _feat_gather(x, g, cid):
    return pl.pallas_call(
        _gather_kernel,
        out_shape=jax.ShapeDtypeStruct((g,) + x.shape, x.dtype),
        in_specs=[pl.BlockSpec(memory_space=pl.ANY)],
        out_specs=pl.BlockSpec(memory_space=pl.ANY),
        scratch_shapes=[pltpu.SemaphoreType.DMA(()), pltpu.SemaphoreType.DMA((g,))],
        compiler_params=pltpu.CompilerParams(has_side_effects=True, collective_id=cid),
    )(x).reshape((g * x.shape[0],) + x.shape[1:])


def per_device(n_dom, n_feat, replica_feat, adjacency_tiles, tile_index, route, node_feat, w_self, w_neigh):
    feat_width, slot_count = replica_feat.shape
    tile_side = adjacency_tiles.shape[1]
    block_count = slot_count // tile_side
    node_count = node_feat.shape[1]
    group = slot_count // n_dom
    full_feat = lax.all_gather(node_feat, "feat", axis=0, tiled=True)
    stacked = replica_feat.reshape(feat_width, block_count, tile_side)
    source = (tile_index[1][:, None] == jnp.arange(block_count, dtype=jnp.int32)[None, :]).astype(
        jnp.bfloat16
    )
    picked = jnp.einsum(
        "fsj,ts->ftj", stacked, source, preferred_element_type=jnp.float32
    ).astype(jnp.bfloat16)
    one_hot = (tile_index[0][:, None] == jnp.arange(block_count, dtype=jnp.int32)[None, :]).astype(
        jnp.float32
    )
    product = jnp.einsum(
        "tij,ftj->tif", adjacency_tiles, picked, preferred_element_type=jnp.float32
    )
    summed = jnp.einsum("tif,tb->bif", product, one_hot, precision=lax.Precision.HIGH)
    paired = summed.astype(jnp.bfloat16)
    half = group // 2
    send = paired.reshape(n_dom, 2, half, feat_width).transpose(0, 2, 1, 3)
    send = send.reshape(n_dom, half, 2 * feat_width)
    got, got_route = _all_to_all([send, route.reshape(n_dom, 1, group)], 0)
    got = got.reshape(slot_count // 2, 2 * feat_width)
    got_route = got_route.reshape(n_dom, 2, half)
    nodes = jnp.arange(node_count, dtype=jnp.int32)[:, None]
    choosers = [
        (got_route[:, parity, :].reshape(1, n_dom * half) == nodes).astype(jnp.bfloat16)
        for parity in range(2)
    ]
    first = (((0,), (0,)), ((), ()))
    agg = sum(
        lax.dot_general(
            got[:, parity * feat_width : (parity + 1) * feat_width],
            choosers[parity],
            (((0,), (1,)), ((), ())),
            preferred_element_type=jnp.float32,
        )
        for parity in range(2)
    ).astype(jnp.bfloat16)
    offset = lax.axis_index("feat") * feat_width
    full_agg = _feat_gather(agg, n_feat, 1)
    self_cols = lax.dynamic_slice_in_dim(w_self, offset, feat_width, 1)
    neigh_cols = lax.dynamic_slice_in_dim(w_neigh, offset, feat_width, 1)
    preact = lax.dot_general(self_cols, full_feat, first, preferred_element_type=jnp.float32)
    preact = preact + lax.dot_general(neigh_cols, full_agg, first, preferred_element_type=jnp.float32)
    renewed = jnp.maximum(preact, jnp.float32(0.0)).astype(jnp.bfloat16)
    picked_rows = [
        lax.dot_general(
            choosers[parity], renewed, (((0,), (1,)), ((), ())), preferred_element_type=jnp.float32
        ).astype(jnp.bfloat16)
        for parity in range(2)
    ]
    back_send = jnp.concatenate(picked_rows, axis=1).reshape(n_dom, group // 2, 2 * feat_width)
    (back,) = _all_to_all([back_send], 2)
    back = back.reshape(n_dom * half, 2 * feat_width)
    row = lax.broadcasted_iota(jnp.int32, (n_dom * half, slot_count), 0)
    col = lax.broadcasted_iota(jnp.int32, (n_dom * half, slot_count), 1)
    home = (row // half) * group + row % half
    replicas = sum(
        lax.dot_general(
            back[:, parity * feat_width : (parity + 1) * feat_width],
            (col == home + parity * half).astype(jnp.bfloat16),
            first,
            preferred_element_type=jnp.float32,
        )
        for parity in range(2)
    ).astype(jnp.bfloat16)
    return (renewed, replicas)


def solution(mesh):
    in_specs = (
        P("feat", "dom"),
        P("dom", None, None),
        P(None, "dom"),
        P(None, "dom"),
        P("feat", "dom"),
        P(),
        P(),
    )
    out_specs = (P("feat", "dom"), P("feat", "dom"))
    body = functools.partial(per_device, mesh.shape["dom"], mesh.shape["feat"])
    return jax.shard_map(body, mesh=mesh, in_specs=in_specs, out_specs=out_specs, check_vma=False)
```
